32 devices in a mesh: groups: 1, ep: 16 (over z, y, x), side: 2 (over core).
Axes of the slice: x: 2, y: 2, z: 4, core: 2. Of those that a mesh axis runs over, the one named last changes fastest.
Arguments:
- queries: bfloat16 [128, 128, 576], P(('groups', 'ep', 'side')), may hold values from -16 to 16
- latent_cache: bfloat16 [64, 128, 576], P(('groups', 'ep', 'side')), may hold values from -16 to 16
- new_latent: bfloat16 [128, 576], P(('groups', 'ep', 'side')), may hold values from -6 to 6
- lengths: int32 [64], P(('groups', 'ep', 'side')), may hold values from 2 to 128
- residual: bfloat16 [128, 3584], P(('groups', 'ep', 'side')), may hold values from -6 to 6
- norm_gain: float32 [3584], replicated, may hold values from 0.5 to 1.5
- value_up: bfloat16 [128, 512, 128], P(('ep', 'side')), may hold values from -0.25 to 0.25
- output_proj: bfloat16 [128, 128, 3584], P(('ep', 'side')), may hold values from -0.1875 to 0.1875
- expert_ids: int32 [128, 8], P(('groups', 'ep', 'side')), may hold values from 0 to 15, all different within a row; in each aligned block of 4 rows (0 to 3, 4 to 7, ...) at most 2 rows name the same one
- expert_weights: float32 [128, 8], P(('groups', 'ep', 'side')), may hold values from 0.05 to 0.4
- gate_proj: bfloat16 [16, 3584, 1024], P('ep', None, 'side'), may hold values from -0.09375 to 0.09375
- up_proj: bfloat16 [16, 3584, 1024], P('ep', None, 'side'), may hold values from -0.09375 to 0.09375
- down_proj: bfloat16 [16, 1024, 3584], P('ep', 'side'), may hold values from -0.1875 to 0.1875
Outputs:
- layer_out: bfloat16 [128, 3584], P(('groups', 'ep', 'side'))
The draws below stay inside these ranges and needn't reach their ends.
Inputs may be any that keep to these rules, and one draw needn't show every extreme that they name: `expert_ids`: each row names 8 different experts. The 4 rows of one device name any one expert at most 2 times, and in every draw some device's rows name some expert exactly 2 times.
All inputs are finite; a program needn't handle non-finite values.
Results may differ from the reference program's by a relative error of at most 0.0056.
Values may be sent and summed in bfloat16 or wider, within the bound.
No kernel may reach another device: no remote copies, remote signals or barrier semaphores. Data moves between devices by JAX's collectives and lax.ppermute only.
A program may use at most 64 MiB of HBM per device.

```python
import math
import jax
import jax.numpy as jnp
import numpy as np
from jax import lax

H = 128
LAT = 512
VH = 128
QKD = 192
D = 3584
FF = 1024
TOP = 8
STEPS = 2
CTX = 128
KD = 576
EXPERTS = 16
TOK_PD = 4
REQS = 64
TOKENS = 128
CAP = 2
N_SIDE = 2


def draw_queries(key, part):
    drawn = jnp.clip(jax.random.normal(jax.random.fold_in(key, 11), (TOKENS, H, KD), jnp.float32), -6.0, 6.0)
    return drawn.astype(jnp.bfloat16)


def draw_latent_cache(key, part):
    drawn = jnp.clip(jax.random.normal(jax.random.fold_in(key, 21), (REQS, CTX, KD), jnp.float32), -6.0, 6.0)
    return drawn.astype(jnp.bfloat16)


def place_ends(values, key, smallest, top_value):
    spot = [jax.random.randint(jax.random.fold_in(key, axis), (), 0, length) for axis, length in enumerate(values.shape)]
    main_axis = values.shape.index(max(values.shape))
    neighbour = spot[:main_axis] + [(spot[main_axis] + 1) % values.shape[main_axis]] + spot[main_axis + 1:]
    return values.at[tuple(spot)].set(smallest).at[tuple(neighbour)].set(top_value)


def block_levels(rng, extent, pieces, low, top_value):
    def one(axis_at, blocks):
        heights = jax.random.uniform(jax.random.fold_in(jax.random.fold_in(rng, 6), axis_at), (blocks,), jnp.float32, low / len(pieces), top_value / len(pieces))
        return jnp.repeat(jnp.exp(heights), extent[axis_at] // blocks).reshape((-1,) + (1,) * (len(extent) - axis_at - 1))

    loudness = one(*pieces[0])
    for cut in pieces[1:]:
        loudness = loudness * one(*cut)
    return loudness


def assign_block(own_key, own, number, rows, amount, top, bound, slope):
    sequence = jax.random.permutation(own_key, amount)
    packed, usual = portions_of(amount, rows * top, bound, slope, True), portions_of(amount, rows * top, bound, slope, False)
    places = jnp.arange(amount)

    def named(sizes, offset_by):
        used = int((sizes > 0).sum())
        fixed = max(1, used // 4)
        passed = fixed + (places - fixed + offset_by * (used - fixed)) % max(1, amount - fixed)
        return jnp.zeros((amount,), jnp.int32).at[sequence[jnp.where(places < fixed, places, passed)]].set(jnp.asarray(sizes, jnp.int32))

    sizes = jnp.where(number % 4 == 0, named(packed, number // 4), named(usual, number - number // 4 - 1))
    mixed = jax.random.permutation(jax.random.fold_in(own, 3), amount)
    donor, taker = mixed[0:amount // 2 * 2:2], mixed[1:amount // 2 * 2:2]
    margin = jnp.minimum(sizes[donor] - 1, bound - sizes[taker]) // 2
    margin = jnp.where((donor == sequence[0]) | (taker == sequence[0]) | (sizes[taker] == 0), 0, jnp.maximum(margin, 0))
    passed = jax.random.randint(jax.random.fold_in(own, 4), (amount // 2,), 0, 1 << 20) % (margin + 1)
    sizes = sizes.at[donor].add(-passed).at[taker].add(passed)
    labels = jnp.searchsorted(jnp.cumsum(sizes), jnp.arange(rows * top), side="right").astype(jnp.int32)
    listing = labels.reshape(top, rows).T
    listing = listing[jax.random.permutation(jax.random.fold_in(own, 1), rows)]
    offset_by = jax.random.randint(jax.random.fold_in(own, 2), (rows, 1), 0, top)
    return jnp.take_along_axis(listing, (jnp.arange(top)[None, :] + offset_by) % top, axis=1)


def portions_of(count, total, most, slope, full):
    loads = [(1 << 20) // math.isqrt(rank ** slope) + 1 for rank in range(1, count + 1)]
    largest = most if full else min(most, max(-(-total // count), total * loads[0] // sum(loads)))
    least = 1 if total - largest >= count - 1 else 0
    given, rest = [largest] + [least] * (count - 1), total - largest - least * (count - 1)
    while rest > 0:
        free = [i for i in range(1, count) if given[i] < largest] or [i for i in range(1, count) if given[i] < most]
        mass, budget = sum([loads[i] for i in free]), rest
        for i in free:
            extra = min(most - given[i], max(1, budget * loads[i] // mass), rest)
            given[i] = given[i] + extra
            rest = rest - extra
    return np.array(given)


def scatter_about(stream_key, extent, spread, most, shards=(), kind=jnp.bfloat16):
    array = jax.random.normal(stream_key, extent, jnp.float32) * spread
    if len(shards) > 0:
        array = block_levels(stream_key, extent, shards, -0.22, 0.18) * array
    return jnp.clip(array, min=-most, max=most).astype(kind)


def setup_inputs(seed: int = 0, part: int = 0) -> dict:
    key_of = jax.random.split(jax.random.key(seed), 14)
    part_keys = jax.random.split(jax.random.fold_in(key_of[13], part), 14)
    queries = draw_queries(jax.random.fold_in(jax.random.fold_in(key_of[13], part), 71), part)
    latent_cache = draw_latent_cache(jax.random.fold_in(jax.random.fold_in(key_of[13], part), 71), part)
    new_latent = scatter_about(part_keys[2], (TOKENS, KD), 1.0, 6.0, ((0, 32),))
    lengths = place_ends(jax.random.randint(part_keys[3], (REQS,), 2, CTX + 1), jax.random.fold_in(part_keys[3], 1), 2, CTX).astype(jnp.int32)
    residual = scatter_about(part_keys[4], (TOKENS, D), 1.0, 6.0, ((0, 32),))
    norm_gain = jnp.clip(1.0 + 0.1 * jax.random.normal(key_of[5], (D,), jnp.float32), 0.5, 1.5)
    value_up = scatter_about(key_of[6], (H, LAT, VH), LAT ** -0.5, 0.25, ((0, 32),))
    output_proj = scatter_about(key_of[7], (H, VH, D), (H * VH // 16) ** -0.5, 0.1875, ((0, 32),))
    expert_ids_keys = jax.random.split(jax.random.fold_in(part_keys[8], 1), TOKENS // TOK_PD)
    expert_ids_turns = jax.random.permutation(jax.random.fold_in(part_keys[8], 3), TOKENS // TOK_PD)
    expert_ids = jax.vmap(lambda own, number: assign_block(jax.random.fold_in(part_keys[8], 2), own, number, TOK_PD, EXPERTS, TOP, CAP, 2))(expert_ids_keys, expert_ids_turns).reshape((TOKENS, TOP))
    expert_weights = jnp.clip(jnp.exp(math.log(0.4) - 2.0794415 * jax.random.uniform(part_keys[9], (TOKENS, TOP), jnp.float32) ** block_levels(part_keys[9], (TOKENS, TOP), ((0, 32),), -0.2, 0.2)), 0.05, 0.4)
    gate_proj = scatter_about(key_of[10], (EXPERTS, D, FF), D ** -0.5, 0.09375, ((0, 16), (2, 2)))
    up_proj = scatter_about(key_of[11], (EXPERTS, D, FF), D ** -0.5, 0.09375, ((0, 16), (2, 2)))
    down_proj = scatter_about(key_of[12], (EXPERTS, FF, D), FF ** -0.5, 0.1875, ((0, 16), (1, 2)))
    return dict(queries=queries, latent_cache=latent_cache, new_latent=new_latent, lengths=lengths, residual=residual, norm_gain=norm_gain, value_up=value_up, output_proj=output_proj, expert_ids=expert_ids, expert_weights=expert_weights, gate_proj=gate_proj, up_proj=up_proj, down_proj=down_proj)


norm_epsilon = 1e-06
masked_score = -1e+30

def latent_attention(query_steps, latent_cache, new_steps, lengths):
    highest = lax.Precision.HIGHEST
    factor = 1.0 / QKD ** 0.5
    query_wide = query_steps.astype(jnp.float32)
    cache_wide = latent_cache.astype(jnp.float32)
    fresh_wide = new_steps.astype(jnp.float32)
    cache_scores = jnp.einsum('rshk,rpk->rshp', query_wide, cache_wide, precision=highest) * factor
    fresh_scores = jnp.einsum('rshk,rqk->rshq', query_wide, fresh_wide, precision=highest) * factor
    cache_live = lax.broadcasted_iota(jnp.int32, cache_scores.shape, 3) < lengths.astype(jnp.int32)[:, None, None, None]
    fresh_live = lax.broadcasted_iota(jnp.int32, fresh_scores.shape, 3) <= lax.broadcasted_iota(jnp.int32, fresh_scores.shape, 1)
    cache_scores = jnp.where(cache_live, cache_scores, masked_score)
    fresh_scores = jnp.where(fresh_live, fresh_scores, masked_score)
    highest_score = jnp.maximum(lax.optimization_barrier(jnp.max(cache_scores, axis=3)), lax.optimization_barrier(jnp.max(fresh_scores, axis=3)))[..., None]
    cache_weight = jnp.where(cache_live, jnp.exp(cache_scores - highest_score), 0.0)
    fresh_weight = jnp.where(fresh_live, jnp.exp(fresh_scores - highest_score), 0.0)
    weight_sum = lax.optimization_barrier(jnp.sum(cache_weight, axis=3)) + lax.optimization_barrier(jnp.sum(fresh_weight, axis=3))
    cache_round = lax.optimization_barrier(cache_weight.astype(jnp.bfloat16)).astype(jnp.float32)
    fresh_round = lax.optimization_barrier(fresh_weight.astype(jnp.bfloat16)).astype(jnp.float32)
    merged = jnp.einsum('rshp,rpl->rshl', cache_round, cache_wide[:, :, :LAT], precision=highest)
    merged = merged + jnp.einsum('rshq,rql->rshl', fresh_round, fresh_wide[:, :, :LAT], precision=highest)
    return (merged / weight_sum[..., None]).astype(jnp.bfloat16)

def reference(queries, latent_cache, new_latent, lengths, residual, norm_gain, value_up, output_proj, expert_ids, expert_weights, gate_proj, up_proj, down_proj):
    highest = lax.Precision.HIGHEST
    query_steps = queries.reshape(REQS, STEPS, H, KD)
    new_steps = new_latent.reshape(REQS, STEPS, KD)
    latent_out = latent_attention(query_steps, latent_cache, new_steps, lengths).reshape(TOKENS, H, LAT)
    head_out = jnp.einsum('thl,hlv->thv', latent_out.astype(jnp.float32), value_up.astype(jnp.float32), precision=highest).astype(jnp.bfloat16)
    attention = jnp.dot(head_out.reshape(TOKENS, H * VH), output_proj.reshape(H * VH, D), preferred_element_type=jnp.float32)
    stream = residual.astype(jnp.float32) + attention
    mean_square = lax.optimization_barrier(jnp.mean(stream * stream, axis=1, keepdims=True))
    normed = (stream * lax.rsqrt(mean_square + norm_epsilon) * norm_gain[None, :]).astype(jnp.bfloat16)
    half_width = FF // N_SIDE
    expert_range = jnp.arange(EXPERTS, dtype=jnp.int32)

    def one_expert(carry, inputs):
        gate_weight, up_weight, down_weight, expert_index = inputs
        share = lax.optimization_barrier(jnp.sum(jnp.where(expert_ids == expert_index, expert_weights, 0.0), axis=1))
        result = jnp.zeros((TOKENS, D), jnp.float32)
        for half in range(N_SIDE):
            lower = half * half_width
            upper = lower + half_width
            gate_part = jnp.dot(normed, gate_weight[:, lower:upper], preferred_element_type=jnp.float32)
            up_part = jnp.dot(normed, up_weight[:, lower:upper], preferred_element_type=jnp.float32)
            hidden = (jax.nn.silu(gate_part) * up_part).astype(jnp.bfloat16)
            partial_value = jnp.dot(hidden, down_weight[lower:upper, :], preferred_element_type=jnp.float32).astype(jnp.bfloat16)
            result = result + lax.optimization_barrier(partial_value).astype(jnp.float32)
        return (carry + share[:, None] * result, None)
    mixture, unused = lax.scan(one_expert, jnp.zeros((TOKENS, D), jnp.float32), (gate_proj, up_proj, down_proj, expert_range))
    return (stream + mixture).astype(jnp.bfloat16)
```

```python
import jax
import jax.numpy as jnp
from jax import lax
from jax.sharding import PartitionSpec as P

LAT = 512
QKD = 192


norm_epsilon = 1e-06
masked_score = -1e30


def attend_block(query_steps, latent_cache, new_steps, lengths):
    factor = 1.0 / QKD**0.5
    cache_scores = (
        jnp.einsum("rshk,rpk->rshp", query_steps, latent_cache, preferred_element_type=jnp.float32)
        * factor
    )
    fresh_scores = (
        jnp.einsum("rshk,rqk->rshq", query_steps, new_steps, preferred_element_type=jnp.float32)
        * factor
    )
    cache_live = (
        lax.broadcasted_iota(jnp.int32, cache_scores.shape, 3) < lengths[:, None, None, None]
    )
    fresh_live = lax.broadcasted_iota(jnp.int32, fresh_scores.shape, 3) <= lax.broadcasted_iota(
        jnp.int32, fresh_scores.shape, 1
    )
    cache_scores = jnp.where(cache_live, cache_scores, masked_score)
    fresh_scores = jnp.where(fresh_live, fresh_scores, masked_score)
    highest_score = jnp.maximum(jnp.max(cache_scores, axis=3), jnp.max(fresh_scores, axis=3))[
        ..., None
    ]
    cache_weight = jnp.where(cache_live, jnp.exp(cache_scores - highest_score), 0.0)
    fresh_weight = jnp.where(fresh_live, jnp.exp(fresh_scores - highest_score), 0.0)
    weight_sum = jnp.sum(cache_weight, axis=3) + jnp.sum(fresh_weight, axis=3)
    merged = jnp.einsum(
        "rshp,rpl->rshl",
        cache_weight.astype(jnp.bfloat16),
        latent_cache[:, :, :LAT],
        preferred_element_type=jnp.float32,
    )
    merged = merged + jnp.einsum(
        "rshq,rql->rshl",
        fresh_weight.astype(jnp.bfloat16),
        new_steps[:, :, :LAT],
        preferred_element_type=jnp.float32,
    )
    return (merged / weight_sum[..., None]).astype(jnp.bfloat16)


def swap_sides(block, shift):
    count = lax.axis_size("side")
    return lax.ppermute(block, "side", [(s, (s + shift) % count) for s in range(count)])


def local(
    queries,
    latent_cache,
    new_latent,
    lengths,
    residual,
    norm_gain,
    value_up,
    output_proj,
    expert_ids,
    expert_weights,
    gate_proj,
    up_proj,
    down_proj,
):
    requests = latent_cache.shape[0]
    positions = queries.shape[0] // requests
    head_count = queries.shape[1]
    feature = residual.shape[1]
    row_count = requests * positions
    ep_count = lax.axis_size("ep")
    side_count = lax.axis_size("side")
    side = lax.axis_index("side")
    own_heads = value_up.shape[0]
    capacity = min(
        row_count, max(2, (row_count * expert_ids.shape[1] + ep_count - 1) // ep_count)
    )
    query_steps = queries.reshape(requests, positions, head_count, queries.shape[2])
    new_steps = new_latent.reshape(requests, positions, new_latent.shape[1])
    flat_out = output_proj.reshape(own_heads * output_proj.shape[1], feature)

    latent = attend_block(query_steps, latent_cache, new_steps, lengths)
    latent = latent.reshape(row_count, head_count, latent.shape[3])
    arrived = lax.all_to_all(latent, ("ep", "side"), split_axis=1, concat_axis=0, tiled=True)
    head_out = jnp.einsum(
        "ngl,glv->ngv", arrived, value_up, preferred_element_type=jnp.float32
    ).astype(jnp.bfloat16)
    head_flat = head_out.reshape(
        ep_count, side_count, row_count, own_heads * head_out.shape[2]
    )

    def project(shift):
        rows = lax.dynamic_index_in_dim(
            head_flat, (side + shift) % side_count, axis=1, keepdims=False
        ).reshape(ep_count * row_count, head_flat.shape[3])
        return jnp.dot(rows, flat_out, preferred_element_type=jnp.float32)

    others = [
        swap_sides(project(shift).astype(jnp.bfloat16), shift) for shift in range(1, side_count)
    ]
    contribution = project(0)
    for other in others:
        contribution = contribution + other.astype(jnp.float32)
    shared = lax.all_to_all(
        contribution.astype(jnp.bfloat16).reshape(ep_count, row_count, feature),
        "ep",
        split_axis=0,
        concat_axis=0,
        tiled=True,
    )
    attention = jnp.sum(shared.astype(jnp.float32), axis=0)
    stream = residual.astype(jnp.float32) + attention
    mean_square = jnp.mean(stream * stream, axis=1, keepdims=True)
    normed = (stream * lax.rsqrt(mean_square + norm_epsilon) * norm_gain[None, :]).astype(
        jnp.bfloat16
    )
    chosen = expert_ids[:, :, None] == lax.broadcasted_iota(jnp.int32, (1, 1, ep_count), 2)
    picked_count = jnp.sum(chosen.astype(jnp.int32), axis=1)
    routed_share = jnp.sum(jnp.where(chosen, expert_weights[:, :, None], 0.0), axis=1)
    before = jnp.cumsum(picked_count, axis=0) - picked_count
    placement = (before[:, :, None] == lax.broadcasted_iota(jnp.int32, (1, 1, capacity), 2)) & (
        picked_count[:, :, None] > 0
    )
    outbound = jnp.einsum(
        "nec,nd->ecd", placement.astype(jnp.bfloat16), normed, preferred_element_type=jnp.float32
    ).astype(jnp.bfloat16)
    own_rows = lax.all_to_all(outbound, "ep", split_axis=0, concat_axis=0, tiled=True).reshape(
        ep_count * capacity, feature
    )
    flat_rows = jnp.concatenate(
        [own_rows] + [swap_sides(own_rows, side_count - shift) for shift in range(1, side_count)]
    )
    gate_part = jnp.dot(flat_rows, gate_proj[0], preferred_element_type=jnp.float32)
    up_part = jnp.dot(flat_rows, up_proj[0], preferred_element_type=jnp.float32)
    hidden = (jax.nn.silu(gate_part) * up_part).astype(jnp.bfloat16)
    partial_value = jnp.dot(hidden, down_proj[0], preferred_element_type=jnp.float32).astype(
        jnp.bfloat16
    )
    partial_value = partial_value.reshape(side_count, ep_count * capacity, feature)
    both = partial_value[0].astype(jnp.float32)
    for shift in range(1, side_count):
        both = both + swap_sides(partial_value[shift], shift).astype(jnp.float32)
    returned = lax.all_to_all(
        both.astype(jnp.bfloat16).reshape(ep_count, capacity, feature),
        "ep",
        split_axis=0,
        concat_axis=0,
        tiled=True,
    )
    coefficient = jnp.where(placement, routed_share[:, :, None], 0.0)
    mixture = jnp.einsum(
        "nec,ecd->nd",
        coefficient,
        returned.astype(jnp.float32),
        precision=lax.Precision.HIGHEST,
    )
    return (stream + mixture).astype(jnp.bfloat16)


def solution(mesh):
    in_specs = (
        P(("groups", "ep", "side"), None, None),
        P(("groups", "ep", "side"), None, None),
        P(("groups", "ep", "side"), None),
        P(("groups", "ep", "side")),
        P(("groups", "ep", "side"), None),
        P(),
        P(("ep", "side"), None, None),
        P(("ep", "side"), None, None),
        P(("groups", "ep", "side"), None),
        P(("groups", "ep", "side"), None),
        P("ep", None, "side"),
        P("ep", None, "side"),
        P("ep", "side", None),
    )
    out_specs = P(("groups", "ep", "side"), None)
    return jax.shard_map(local, mesh=mesh, in_specs=in_specs, out_specs=out_specs, check_vma=False)
```

```python
import functools

import jax
import jax.numpy as jnp
from jax import lax
from jax.experimental import pallas as pl
from jax.experimental.pallas import tpu as pltpu
from jax.sharding import PartitionSpec as P

LAT = 512
QKD = 192
LANES = 128


norm_epsilon = 1e-06
masked_score = -1e30

VMEM_SPEC = pl.BlockSpec(memory_space=pltpu.VMEM)
HBM_SPEC = pl.BlockSpec(memory_space=pltpu.HBM)


def stay(array):
    return pltpu.with_memory_space_constraint(array, pltpu.HBM)


def place(array):
    return pltpu.with_memory_space_constraint(array, pltpu.VMEM)


def attention_kernel(
    lengths_hbm,
    queries_hbm,
    cache_hbm,
    fresh_hbm,
    up_hbm,
    project_hbm,
    out_ref,
    up_ref,
    project_ref,
    lengths_ref,
    queries_ref,
    cache_ref,
    fresh_ref,
    rows_ref,
    placed_ref,
    sems,
):
    requests = cache_hbm.shape[0]
    positions = queries_hbm.shape[0] // requests
    first = [
        pltpu.make_async_copy(lengths_hbm, lengths_ref, sems.at[0]),
        pltpu.make_async_copy(fresh_hbm, fresh_ref, sems.at[1]),
    ]
    pieces = []
    for r in range(requests):
        tokens_of = pl.ds(r * positions, positions)
        pieces.append(
            [
                pltpu.make_async_copy(cache_hbm.at[r], cache_ref.at[r], sems.at[2 + 2 * r]),
                pltpu.make_async_copy(
                    queries_hbm.at[tokens_of], queries_ref.at[tokens_of], sems.at[3 + 2 * r]
                ),
            ]
        )
    count = 2 + 2 * requests
    loads = [
        pltpu.make_async_copy(up_hbm, up_ref, sems.at[count]),
        pltpu.make_async_copy(project_hbm, project_ref, sems.at[count + 1]),
    ]
    for copy in first + sum(pieces, []) + loads:
        copy.start()
    for copy in first:
        copy.wait()
    factor = 1.0 / QKD**0.5
    tokens, _, heads = queries_ref.shape
    holders, block, latent_width = out_ref.shape
    own_heads = block // tokens
    fresh_rows = -(-positions // 8) * 8
    for r in range(requests):
        for copy in pieces[r]:
            copy.wait()
        keys = jnp.transpose(cache_ref[r])
        wanted = jnp.concatenate(
            [queries_ref[r * positions + j] for j in range(positions)], axis=1
        )
        fresh = fresh_ref[r * positions : (r + 1) * positions, :]
        cache_scores = jnp.dot(keys, wanted, preferred_element_type=jnp.float32) * factor
        padded = jnp.concatenate(
            [fresh, jnp.zeros((16 - positions, fresh.shape[1]), fresh.dtype)], axis=0
        )
        fresh_scores = (
            jnp.dot(padded, wanted, preferred_element_type=jnp.float32)[:fresh_rows] * factor
        )
        cache_live = lax.broadcasted_iota(jnp.int32, cache_scores.shape, 0) < lengths_ref[r]
        fresh_row = lax.broadcasted_iota(jnp.int32, fresh_scores.shape, 0)
        step = lax.broadcasted_iota(jnp.int32, fresh_scores.shape, 1) // heads
        fresh_live = fresh_row <= step
        cache_scores = jnp.where(cache_live, cache_scores, masked_score)
        fresh_scores = jnp.where(fresh_live, fresh_scores, masked_score)
        highest = jnp.maximum(
            jnp.max(cache_scores, axis=0, keepdims=True),
            jnp.max(fresh_scores, axis=0, keepdims=True),
        )
        cache_weight = jnp.where(cache_live, jnp.exp(cache_scores - highest), 0.0)
        fresh_weight = jnp.where(fresh_live, jnp.exp(fresh_scores - highest), 0.0)
        total = jnp.sum(cache_weight, axis=0, keepdims=True) + jnp.sum(
            fresh_weight, axis=0, keepdims=True
        )
        side_columns = jnp.where(fresh_row == positions, total, fresh_weight)
        for j in range(positions):
            lanes = slice(j * heads, (j + 1) * heads)
            columns = jnp.transpose(side_columns[:, lanes])
            weights = jnp.transpose(cache_weight[:, lanes]).astype(jnp.bfloat16)
            merged = jnp.dot(
                weights, keys[:, :latent_width], preferred_element_type=jnp.float32
            )
            for q in range(j + 1):
                merged = merged + columns[:, q : q + 1].astype(jnp.bfloat16).astype(
                    jnp.float32
                ) * fresh[q : q + 1, :latent_width].astype(jnp.float32)
            merged = merged / columns[:, positions : positions + 1]
            token = r * positions + j
            for part in range(latent_width // LANES):
                rows_ref[part] = merged[:, part * LANES : (part + 1) * LANES]
                for i in range(own_heads):
                    placed_ref[part, pl.ds(token * own_heads + i, holders, stride=block), :] = (
                        rows_ref[part, pl.ds(i, holders, stride=own_heads), :]
                    )
    for part in range(latent_width // LANES):
        out_ref[:, :, part * LANES : (part + 1) * LANES] = (
            placed_ref[part].astype(jnp.bfloat16).reshape(holders, block, LANES)
        )
    for copy in loads:
        copy.wait()


def attend(queries, latent_cache, new_latent, lengths, value_up, flat_out, holders):
    tokens, heads, _ = queries.shape
    requests = latent_cache.shape[0]
    block = tokens * heads // holders
    operands = (lengths, jnp.swapaxes(queries, 1, 2), jnp.swapaxes(latent_cache, 1, 2), new_latent)
    return pl.pallas_call(
        attention_kernel,
        out_shape=[
            jax.ShapeDtypeStruct((holders, block, LAT), jnp.bfloat16),
            pltpu.VMEM(value_up.shape, value_up.dtype),
            pltpu.VMEM(flat_out.shape, flat_out.dtype),
        ],
        in_specs=[HBM_SPEC] * 6,
        out_specs=[VMEM_SPEC] * 3,
        scratch_shapes=[pltpu.SMEM(lengths.shape, lengths.dtype)]
        + [pltpu.VMEM(x.shape, x.dtype) for x in operands[1:]]
        + [
            pltpu.VMEM((LAT // LANES, heads, LANES), jnp.float32),
            pltpu.VMEM((LAT // LANES, tokens * heads, LANES), jnp.float32),
            pltpu.SemaphoreType.DMA((4 + 2 * requests,)),
        ],
        compiler_params=pltpu.CompilerParams(vmem_limit_bytes=16 << 20),
    )(*map(stay, operands + (value_up, flat_out)))


def column_step(width):
    for step in (512, 384, 256, 128):
        if width % step == 0:
            return step
    return width


def head_kernel(
    arrived_ref, up_ref, out_ref, gate_hbm, send_ref, own_ref, gate_ref, wide_ref, sem
):
    load = pltpu.make_async_copy(gate_hbm, gate_ref, sem)
    load.start()
    tokens_in = arrived_ref.shape[1] // up_ref.shape[0]
    sources, block, latent_width = arrived_ref.shape
    own_heads, _, value_width = up_ref.shape
    step = column_step(out_ref.shape[1])
    steps = out_ref.shape[1] // step
    rows = sources * tokens_in
    parts = latent_width // LANES
    for part in range(parts):
        wide_ref[part] = (
            arrived_ref[:, :, part * LANES : (part + 1) * LANES]
            .reshape(sources * block, LANES)
            .astype(jnp.float32)
        )
    outs = []
    for i in range(own_heads):
        latent = jnp.concatenate(
            [
                wide_ref[part, pl.ds(i, rows, stride=own_heads), :].astype(jnp.bfloat16)
                for part in range(parts)
            ],
            axis=1,
        )
        outs.append(
            jnp.dot(latent, up_ref[i], preferred_element_type=jnp.float32).astype(jnp.bfloat16)
        )
    heads = jnp.concatenate(outs, axis=1)
    side = lax.axis_index("side")
    half = rows // 2
    target = lax.broadcasted_iota(jnp.int32, (rows, rows), 0)
    source = lax.broadcasted_iota(jnp.int32, (rows, rows), 1)
    within = jnp.where(target < half, target, target - half)
    wanted_side = jnp.where(target < half, side, 1 - side)
    origin = (within // tokens_in) * (2 * tokens_in) + wanted_side * tokens_in + within % tokens_in
    sorter = jnp.where(source == origin, 1.0, 0.0).astype(jnp.bfloat16)
    ordered = jnp.dot(sorter, heads, preferred_element_type=jnp.float32).astype(jnp.bfloat16)
    own_ref[...] = ordered[:half]
    other = ordered[half:]
    for k in range(steps):
        columns = slice(k * step, (k + 1) * step)
        send_ref[:, columns] = jnp.dot(
            other, out_ref[:, columns], preferred_element_type=jnp.float32
        ).astype(jnp.bfloat16)
    load.wait()


def project_heads(arrived, value_up, flat_out, gate):
    sources, block, _ = arrived.shape
    own_heads, latent_width, value_width = value_up.shape
    half = sources * block // own_heads // 2
    feature = flat_out.shape[1]
    return pl.pallas_call(
        head_kernel,
        out_shape=[
            jax.ShapeDtypeStruct((half, feature), jnp.bfloat16),
            jax.ShapeDtypeStruct((half, own_heads * value_width), jnp.bfloat16),
            pltpu.VMEM(gate.shape, gate.dtype),
        ],
        in_specs=[VMEM_SPEC] * 3 + [HBM_SPEC],
        out_specs=[VMEM_SPEC] * 3,
        scratch_shapes=[
            pltpu.VMEM((latent_width // LANES, sources * block, LANES), jnp.float32),
            pltpu.SemaphoreType.DMA,
        ],
        compiler_params=pltpu.CompilerParams(vmem_limit_bytes=16 << 20),
    )(place(arrived), place(value_up), place(flat_out), stay(gate))


def own_kernel(heads_ref, out_ref, up_hbm, keep_ref, up_ref, sem):
    load = pltpu.make_async_copy(up_hbm, up_ref, sem)
    load.start()
    step = column_step(out_ref.shape[1])
    for k in range(out_ref.shape[1] // step):
        columns = slice(k * step, (k + 1) * step)
        keep_ref[:, columns] = jnp.dot(
            heads_ref[...], out_ref[:, columns], preferred_element_type=jnp.float32
        )
    load.wait()


def project_own(heads, flat_out, up):
    rows, feature = heads.shape[0], flat_out.shape[1]
    return pl.pallas_call(
        own_kernel,
        out_shape=[
            jax.ShapeDtypeStruct((rows, feature), jnp.float32),
            pltpu.VMEM(up.shape, up.dtype),
        ],
        in_specs=[VMEM_SPEC] * 2 + [HBM_SPEC],
        out_specs=[VMEM_SPEC] * 2,
        scratch_shapes=[pltpu.SemaphoreType.DMA],
        compiler_params=pltpu.CompilerParams(vmem_limit_bytes=4 << 20),
        cost_estimate=pl.CostEstimate(
            flops=2 * rows * flat_out.size,
            bytes_accessed=2 * flat_out.size + 2 * up.size,
            transcendentals=0,
        ),
    )(place(heads), place(flat_out), stay(up))


def sum_kernel(keep_ref, other_ref, out_ref):
    groups, rows, feature = out_ref.shape
    step = column_step(feature)
    for k in range(feature // step):
        columns = slice(k * step, (k + 1) * step)
        total = keep_ref[:, columns].astype(jnp.float32) + other_ref[:, columns].astype(
            jnp.float32
        )
        out_ref[:, :, columns] = total.astype(jnp.bfloat16).reshape(groups, rows, step)


def sum_halves(keep, other, groups):
    count, feature = keep.shape
    return pl.pallas_call(
        sum_kernel,
        out_shape=jax.ShapeDtypeStruct((groups, count // groups, feature), jnp.bfloat16),
        in_specs=[VMEM_SPEC] * 2,
        out_specs=VMEM_SPEC,
        compiler_params=pltpu.CompilerParams(vmem_limit_bytes=4 << 20),
    )(place(keep), place(other))


def stream_kernel(
    shared_ref,
    residual_ref,
    gain_ref,
    ids_ref,
    share_ref,
    rows_ref,
    stream_ref,
    coefficient_ref,
):
    tokens, feature = residual_ref.shape
    experts, capacity, _ = rows_ref.shape
    slots = coefficient_ref.shape[1]
    step = column_step(feature)
    blocks = [slice(k * step, (k + 1) * step) for k in range(feature // step)]
    square = jnp.zeros((tokens, 1), jnp.float32)
    for columns in blocks:
        attention = jnp.sum(shared_ref[:, :, columns].astype(jnp.float32), axis=0)
        stream = residual_ref[:, columns].astype(jnp.float32) + attention
        stream_ref[:, columns] = stream
        square = square + jnp.sum(stream * stream, axis=1, keepdims=True)
    scale = lax.rsqrt(square / feature + norm_epsilon)

    slot = lax.broadcasted_iota(jnp.int32, (tokens, slots), 1)
    expert = slot // capacity
    row = lax.broadcasted_iota(jnp.int32, (tokens, slots), 0)
    picked = jnp.zeros((tokens, slots), jnp.int32)
    share = jnp.zeros((tokens, slots), jnp.float32)
    for k in range(ids_ref.shape[1]):
        same = ids_ref[:, k : k + 1] == expert
        picked = picked + jnp.where(same, 1, 0)
        share = share + jnp.where(same, share_ref[:, k : k + 1], 0.0)
    before = jnp.zeros((tokens, slots), jnp.int32)
    for t in range(tokens - 1):
        before = before + jnp.where(row > t, picked[t : t + 1, :], 0)
    placed = (picked > 0) & (before == slot % capacity)
    coefficient_ref[...] = jnp.where(placed, share, 0.0)
    padded = jnp.concatenate(
        [jnp.where(placed, 1.0, 0.0), jnp.zeros((8 - tokens, slots), jnp.float32)], axis=0
    )
    chooser = jnp.transpose(padded)[: experts * capacity].astype(jnp.bfloat16)
    for columns in blocks:
        gain = jnp.concatenate(
            [
                gain_ref[part : part + 1, :]
                for part in range(columns.start // LANES, columns.stop // LANES)
            ],
            axis=1,
        )
        normed = stream_ref[:, columns] * scale * gain
        normed = jnp.concatenate(
            [normed, jnp.zeros((8 - tokens, step), jnp.float32)], axis=0
        ).astype(jnp.bfloat16)
        chosen = jnp.dot(chooser, normed, preferred_element_type=jnp.float32)
        rows_ref[:, :, columns] = chosen.astype(jnp.bfloat16).reshape(experts, capacity, step)


def route(shared, residual, gain, expert_ids, expert_weights, capacity):
    experts, tokens, feature = shared.shape
    slots = -(-experts * capacity // LANES) * LANES
    return pl.pallas_call(
        stream_kernel,
        out_shape=[
            jax.ShapeDtypeStruct((experts, capacity, feature), jnp.bfloat16),
            jax.ShapeDtypeStruct((tokens, feature), jnp.float32),
            jax.ShapeDtypeStruct((tokens, slots), jnp.float32),
        ],
        in_specs=[VMEM_SPEC] * 5,
        out_specs=[VMEM_SPEC] * 3,
        compiler_params=pltpu.CompilerParams(vmem_limit_bytes=4 << 20),
    )(place(shared), residual, gain.reshape(feature // LANES, LANES), expert_ids, expert_weights)


def mix_kernel(returned_ref, coefficient_ref, stream_ref, out_ref):
    experts, capacity, feature = returned_ref.shape
    tokens = stream_ref.shape[0]
    count = experts * capacity
    rest = coefficient_ref[:, :count]
    terms = []
    for _ in range(3):
        term = rest.astype(jnp.bfloat16).astype(jnp.float32)
        rest = rest - term
        terms.append(term)
    terms.append(jnp.zeros_like(rest))
    weights = jnp.concatenate(terms, axis=0).astype(jnp.bfloat16)
    step = column_step(feature)
    for k in range(feature // step):
        columns = slice(k * step, (k + 1) * step)
        parts = jnp.dot(
            weights,
            returned_ref[:, :, columns].reshape(count, step),
            preferred_element_type=jnp.float32,
        )
        mixture = parts[:tokens] + parts[tokens : 2 * tokens] + parts[2 * tokens : 3 * tokens]
        out_ref[:, columns] = (stream_ref[:, columns] + mixture).astype(jnp.bfloat16)


def mix(returned, coefficient, stream):
    return pl.pallas_call(
        mix_kernel,
        out_shape=jax.ShapeDtypeStruct(stream.shape, jnp.bfloat16),
        in_specs=[VMEM_SPEC] * 3,
        out_specs=VMEM_SPEC,
        compiler_params=pltpu.CompilerParams(vmem_limit_bytes=4 << 20),
    )(place(returned), place(coefficient), place(stream))


def expert_kernel(
    own_rows_ref,
    other_rows_ref,
    gate_ref,
    up_ref,
    down_hbm,
    keep_ref,
    send_ref,
    down_ref,
    hidden_ref,
    sem,
):
    load = pltpu.make_async_copy(down_hbm, down_ref, sem)
    load.start()
    width = gate_ref.shape[1]
    feature = down_hbm.shape[1]
    hidden_step = 256 if width % 256 == 0 else width
    step = column_step(feature)
    shape = own_rows_ref.shape
    own_count = shape[0] * shape[1]
    rows = jnp.concatenate(
        [
            own_rows_ref[...].reshape(own_count, shape[2]),
            other_rows_ref[...].reshape(own_count, shape[2]),
        ]
    )
    for k in range(width // hidden_step):
        columns = slice(k * hidden_step, (k + 1) * hidden_step)
        gate_part = jnp.dot(rows, gate_ref[:, columns], preferred_element_type=jnp.float32)
        up_part = jnp.dot(rows, up_ref[:, columns], preferred_element_type=jnp.float32)
        hidden_ref[:, columns] = (gate_part / (1.0 + jnp.exp(-gate_part)) * up_part).astype(
            jnp.bfloat16
        )
    hidden = hidden_ref[...]
    load.wait()
    for k in range(feature // step):
        columns = slice(k * step, (k + 1) * step)
        out = jnp.dot(hidden, down_ref[:, columns], preferred_element_type=jnp.float32).astype(
            jnp.bfloat16
        )
        keep_ref[:, columns] = out[:own_count]
        send_ref[:, columns] = out[own_count:]


def expert_halves(own_rows, other_rows, gate, up, down):
    count, feature = own_rows.shape[0] * own_rows.shape[1], own_rows.shape[2]
    return pl.pallas_call(
        expert_kernel,
        out_shape=[jax.ShapeDtypeStruct((count, feature), jnp.bfloat16)] * 2,
        in_specs=[VMEM_SPEC] * 4 + [HBM_SPEC],
        out_specs=[VMEM_SPEC] * 2,
        scratch_shapes=[
            pltpu.VMEM(down.shape, down.dtype),
            pltpu.VMEM((2 * count, gate.shape[1]), jnp.bfloat16),
            pltpu.SemaphoreType.DMA,
        ],
        compiler_params=pltpu.CompilerParams(vmem_limit_bytes=16 << 20),
    )(place(own_rows), place(other_rows), place(gate), place(up), stay(down))


def swap_sides(block):
    return lax.ppermute(block, "side", [(0, 1), (1, 0)])


def local(
    queries,
    latent_cache,
    new_latent,
    lengths,
    residual,
    norm_gain,
    value_up,
    output_proj,
    expert_ids,
    expert_weights,
    gate_proj,
    up_proj,
    down_proj,
):
    row_count = queries.shape[0]
    feature = residual.shape[1]
    ep_count = lax.axis_size("ep")
    side_count = lax.axis_size("side")
    assert side_count == 2
    flat_out = output_proj.reshape(output_proj.shape[0] * output_proj.shape[1], feature)
    capacity = min(
        row_count, max(2, (row_count * expert_ids.shape[1] + ep_count - 1) // ep_count)
    )

    latent, value_up, flat_out = attend(
        queries, latent_cache, new_latent, lengths, value_up, flat_out, ep_count * side_count
    )
    arrived = lax.all_to_all(latent, ("ep", "side"), split_axis=0, concat_axis=0, tiled=True)
    send, own_heads, gate = project_heads(arrived, value_up, flat_out, gate_proj[0])
    from_other = swap_sides(send)
    keep, up = project_own(own_heads, flat_out, up_proj[0])
    contribution = sum_halves(keep, from_other, ep_count)
    shared = lax.all_to_all(contribution, "ep", split_axis=0, concat_axis=0, tiled=True)
    outbound, stream, coefficient = route(
        shared, residual, norm_gain, expert_ids, expert_weights, capacity
    )
    own_rows = lax.all_to_all(outbound, "ep", split_axis=0, concat_axis=0, tiled=True)
    other_rows = swap_sides(own_rows)
    keep, send = expert_halves(own_rows, other_rows, gate, up, down_proj[0])
    both = sum_halves(keep, swap_sides(send), ep_count)
    returned = lax.all_to_all(both, "ep", split_axis=0, concat_axis=0, tiled=True)
    return mix(returned, coefficient, stream)


def solution(mesh):
    in_specs = (
        P(("groups", "ep", "side"), None, None),
        P(("groups", "ep", "side"), None, None),
        P(("groups", "ep", "side"), None),
        P(("groups", "ep", "side")),
        P(("groups", "ep", "side"), None),
        P(),
        P(("ep", "side"), None, None),
        P(("ep", "side"), None, None),
        P(("groups", "ep", "side"), None),
        P(("groups", "ep", "side"), None),
        P("ep", None, "side"),
        P("ep", None, "side"),
        P("ep", "side", None),
    )
    out_specs = P(("groups", "ep", "side"), None)
    return jax.shard_map(local, mesh=mesh, in_specs=in_specs, out_specs=out_specs, check_vma=False)
```

```python
import functools

import jax
import jax.numpy as jnp
from jax import lax
from jax.experimental import pallas as pl
from jax.experimental.pallas import tpu as pltpu
from jax.sharding import PartitionSpec as P

LAT = 512
QKD = 192
LANES = 128


norm_epsilon = 1e-06
masked_score = -1e30

VMEM_SPEC = pl.BlockSpec(memory_space=pltpu.VMEM)
HBM_SPEC = pl.BlockSpec(memory_space=pltpu.HBM)


def stay(array):
    return pltpu.with_memory_space_constraint(array, pltpu.HBM)


def place(array):
    return pltpu.with_memory_space_constraint(array, pltpu.VMEM)


def attention_kernel(
    lengths_hbm,
    queries_hbm,
    cache_hbm,
    fresh_hbm,
    up_hbm,
    project_hbm,
    out_ref,
    up_ref,
    project_ref,
    lengths_ref,
    queries_ref,
    cache_ref,
    fresh_ref,
    rows_ref,
    placed_ref,
    sems,
):
    requests = cache_hbm.shape[0]
    positions = queries_hbm.shape[0] // requests
    first = [
        pltpu.make_async_copy(lengths_hbm, lengths_ref, sems.at[0]),
        pltpu.make_async_copy(fresh_hbm, fresh_ref, sems.at[1]),
    ]
    pieces = []
    for r in range(requests):
        tokens_of = pl.ds(r * positions, positions)
        pieces.append(
            [
                pltpu.make_async_copy(cache_hbm.at[r], cache_ref.at[r], sems.at[2 + 2 * r]),
                pltpu.make_async_copy(
                    queries_hbm.at[tokens_of], queries_ref.at[tokens_of], sems.at[3 + 2 * r]
                ),
            ]
        )
    count = 2 + 2 * requests
    loads = [
        pltpu.make_async_copy(up_hbm, up_ref, sems.at[count]),
        pltpu.make_async_copy(project_hbm, project_ref, sems.at[count + 1]),
    ]
    for copy in first + sum(pieces, []) + loads:
        copy.start()
    for copy in first:
        copy.wait()
    factor = 1.0 / QKD**0.5
    tokens, _, heads = queries_ref.shape
    holders, block, latent_width = out_ref.shape
    own_heads = block // tokens
    fresh_rows = -(-positions // 8) * 8
    for r in range(requests):
        for copy in pieces[r]:
            copy.wait()
        keys = jnp.transpose(cache_ref[r])
        wanted = jnp.concatenate(
            [queries_ref[r * positions + j] for j in range(positions)], axis=1
        )
        fresh = fresh_ref[r * positions : (r + 1) * positions, :]
        cache_scores = jnp.dot(keys, wanted, preferred_element_type=jnp.float32) * factor
        padded = jnp.concatenate(
            [fresh, jnp.zeros((16 - positions, fresh.shape[1]), fresh.dtype)], axis=0
        )
        fresh_scores = (
            jnp.dot(padded, wanted, preferred_element_type=jnp.float32)[:fresh_rows] * factor
        )
        cache_live = lax.broadcasted_iota(jnp.int32, cache_scores.shape, 0) < lengths_ref[r]
        fresh_row = lax.broadcasted_iota(jnp.int32, fresh_scores.shape, 0)
        step = lax.broadcasted_iota(jnp.int32, fresh_scores.shape, 1) // heads
        fresh_live = fresh_row <= step
        cache_scores = jnp.where(cache_live, cache_scores, masked_score)
        fresh_scores = jnp.where(fresh_live, fresh_scores, masked_score)
        highest = jnp.maximum(
            jnp.max(cache_scores, axis=0, keepdims=True),
            jnp.max(fresh_scores, axis=0, keepdims=True),
        )
        cache_weight = jnp.where(cache_live, jnp.exp(cache_scores - highest), 0.0)
        fresh_weight = jnp.where(fresh_live, jnp.exp(fresh_scores - highest), 0.0)
        total = jnp.sum(cache_weight, axis=0, keepdims=True) + jnp.sum(
            fresh_weight, axis=0, keepdims=True
        )
        side_columns = jnp.where(fresh_row == positions, total, fresh_weight)
        for j in range(positions):
            lanes = slice(j * heads, (j + 1) * heads)
            columns = jnp.transpose(side_columns[:, lanes])
            weights = jnp.transpose(cache_weight[:, lanes]).astype(jnp.bfloat16)
            merged = jnp.dot(
                weights, keys[:, :latent_width], preferred_element_type=jnp.float32
            )
            for q in range(j + 1):
                merged = merged + columns[:, q : q + 1].astype(jnp.bfloat16).astype(
                    jnp.float32
                ) * fresh[q : q + 1, :latent_width].astype(jnp.float32)
            merged = merged / columns[:, positions : positions + 1]
            token = r * positions + j
            for part in range(latent_width // LANES):
                rows_ref[part] = merged[:, part * LANES : (part + 1) * LANES]
                for i in range(own_heads):
                    placed_ref[part, pl.ds(token * own_heads + i, holders, stride=block), :] = (
                        rows_ref[part, pl.ds(i, holders, stride=own_heads), :]
                    )
    for part in range(latent_width // LANES):
        out_ref[:, :, part * LANES : (part + 1) * LANES] = (
            placed_ref[part].astype(jnp.bfloat16).reshape(holders, block, LANES)
        )
    for copy in loads:
        copy.wait()


def attend(queries, latent_cache, new_latent, lengths, value_up, flat_out, holders):
    tokens, heads, _ = queries.shape
    requests = latent_cache.shape[0]
    block = tokens * heads // holders
    operands = (lengths, jnp.swapaxes(queries, 1, 2), jnp.swapaxes(latent_cache, 1, 2), new_latent)
    return pl.pallas_call(
        attention_kernel,
        out_shape=[
            jax.ShapeDtypeStruct((holders, block, LAT), jnp.bfloat16),
            pltpu.VMEM(value_up.shape, value_up.dtype),
            pltpu.VMEM(flat_out.shape, flat_out.dtype),
        ],
        in_specs=[HBM_SPEC] * 6,
        out_specs=[VMEM_SPEC] * 3,
        scratch_shapes=[pltpu.SMEM(lengths.shape, lengths.dtype)]
        + [pltpu.VMEM(x.shape, x.dtype) for x in operands[1:]]
        + [
            pltpu.VMEM((LAT // LANES, heads, LANES), jnp.float32),
            pltpu.VMEM((LAT // LANES, tokens * heads, LANES), jnp.float32),
            pltpu.SemaphoreType.DMA((4 + 2 * requests,)),
        ],
        compiler_params=pltpu.CompilerParams(vmem_limit_bytes=16 << 20),
    )(*map(stay, operands + (value_up, flat_out)))


def column_step(width):
    for step in (512, 384, 256, 128):
        if width % step == 0:
            return step
    return width


def head_kernel(
    arrived_ref, up_ref, out_ref, gate_hbm, send_ref, own_ref, gate_ref, wide_ref, sem
):
    load = pltpu.make_async_copy(gate_hbm, gate_ref, sem)
    load.start()
    tokens_in = arrived_ref.shape[1] // up_ref.shape[0]
    sources, block, latent_width = arrived_ref.shape
    own_heads, _, value_width = up_ref.shape
    step = column_step(out_ref.shape[1])
    steps = out_ref.shape[1] // step
    rows = sources * tokens_in
    parts = latent_width // LANES
    for part in range(parts):
        wide_ref[part] = (
            arrived_ref[:, :, part * LANES : (part + 1) * LANES]
            .reshape(sources * block, LANES)
            .astype(jnp.float32)
        )
    outs = []
    for i in range(own_heads):
        latent = jnp.concatenate(
            [
                wide_ref[part, pl.ds(i, rows, stride=own_heads), :].astype(jnp.bfloat16)
                for part in range(parts)
            ],
            axis=1,
        )
        outs.append(
            jnp.dot(latent, up_ref[i], preferred_element_type=jnp.float32).astype(jnp.bfloat16)
        )
    heads = jnp.concatenate(outs, axis=1)
    side = lax.axis_index("side")
    half = rows // 2
    target = lax.broadcasted_iota(jnp.int32, (rows, rows), 0)
    source = lax.broadcasted_iota(jnp.int32, (rows, rows), 1)
    within = jnp.where(target < half, target, target - half)
    wanted_side = jnp.where(target < half, side, 1 - side)
    zone = (within // tokens_in) % 2
    member = within // (2 * tokens_in)
    chip = zone * (half // (2 * tokens_in)) + member
    origin = chip * (2 * tokens_in) + wanted_side * tokens_in + within % tokens_in
    sorter = jnp.where(source == origin, 1.0, 0.0).astype(jnp.bfloat16)
    ordered = jnp.dot(sorter, heads, preferred_element_type=jnp.float32).astype(jnp.bfloat16)
    own_ref[...] = ordered[:half]
    other = ordered[half:]
    for k in range(steps):
        columns = slice(k * step, (k + 1) * step)
        send_ref[:, columns] = jnp.dot(
            other, out_ref[:, columns], preferred_element_type=jnp.float32
        ).astype(jnp.bfloat16)
    load.wait()


def project_heads(arrived, value_up, flat_out, gate):
    sources, block, _ = arrived.shape
    own_heads, latent_width, value_width = value_up.shape
    half = sources * block // own_heads // 2
    feature = flat_out.shape[1]
    return pl.pallas_call(
        head_kernel,
        out_shape=[
            jax.ShapeDtypeStruct((half, feature), jnp.bfloat16),
            jax.ShapeDtypeStruct((half, own_heads * value_width), jnp.bfloat16),
            pltpu.VMEM(gate.shape, gate.dtype),
        ],
        in_specs=[VMEM_SPEC] * 3 + [HBM_SPEC],
        out_specs=[VMEM_SPEC] * 3,
        scratch_shapes=[
            pltpu.VMEM((latent_width // LANES, sources * block, LANES), jnp.float32),
            pltpu.SemaphoreType.DMA,
        ],
        compiler_params=pltpu.CompilerParams(vmem_limit_bytes=16 << 20),
    )(place(arrived), place(value_up), place(flat_out), stay(gate))


def own_kernel(heads_ref, out_ref, up_hbm, keep_ref, up_ref, sem):
    load = pltpu.make_async_copy(up_hbm, up_ref, sem)
    load.start()
    step = column_step(out_ref.shape[1])
    for k in range(out_ref.shape[1] // step):
        columns = slice(k * step, (k + 1) * step)
        keep_ref[:, columns] = jnp.dot(
            heads_ref[...], out_ref[:, columns], preferred_element_type=jnp.float32
        )
    load.wait()


def project_own(heads, flat_out, up):
    rows, feature = heads.shape[0], flat_out.shape[1]
    return pl.pallas_call(
        own_kernel,
        out_shape=[
            jax.ShapeDtypeStruct((rows, feature), jnp.float32),
            pltpu.VMEM(up.shape, up.dtype),
        ],
        in_specs=[VMEM_SPEC] * 2 + [HBM_SPEC],
        out_specs=[VMEM_SPEC] * 2,
        scratch_shapes=[pltpu.SemaphoreType.DMA],
        compiler_params=pltpu.CompilerParams(vmem_limit_bytes=4 << 20),
        cost_estimate=pl.CostEstimate(
            flops=2 * rows * flat_out.size,
            bytes_accessed=2 * flat_out.size + 2 * up.size,
            transcendentals=0,
        ),
    )(place(heads), place(flat_out), stay(up))


def sum_kernel(zones, keep_ref, other_ref, out_ref):
    groups, rows, feature = out_ref.shape
    members = groups // zones
    step = column_step(feature)
    for k in range(feature // step):
        columns = slice(k * step, (k + 1) * step)
        total = keep_ref[:, columns].astype(jnp.float32) + other_ref[:, columns].astype(
            jnp.float32
        )
        total = total.astype(jnp.bfloat16).reshape(groups, rows, step)
        if zones == 1:
            out_ref[:, :, columns] = total
        else:
            for group in range(groups):
                out_ref[group % zones * members + group // zones, :, columns] = total[group]


def sum_halves(keep, other, groups, zones):
    count, feature = keep.shape
    return pl.pallas_call(
        functools.partial(sum_kernel, zones),
        out_shape=jax.ShapeDtypeStruct((groups, count // groups, feature), jnp.bfloat16),
        in_specs=[VMEM_SPEC] * 2,
        out_specs=VMEM_SPEC,
        compiler_params=pltpu.CompilerParams(vmem_limit_bytes=4 << 20),
    )(place(keep), place(other))


def own_zone():
    return lax.axis_index("ep") // (lax.axis_size("ep") // 2)


def fold_kernel(shared_ref, residual_ref, ids_ref, part_ref, send_ref):
    tokens, feature = residual_ref.shape
    rows = 2 * tokens
    mine = lax.broadcasted_iota(jnp.int32, (rows, 1), 0) // tokens == own_zone()
    step = column_step(feature)
    for k in range(feature // step):
        columns = slice(k * step, (k + 1) * step)
        part = jnp.sum(shared_ref[:, :, columns].astype(jnp.float32), axis=0)
        residual = residual_ref[:, columns].astype(jnp.float32)
        part = part + jnp.where(mine, jnp.concatenate([residual, residual], axis=0), 0.0)
        part_ref[:, columns] = part
        send_ref[:, columns] = part.astype(jnp.bfloat16)
    ids = ids_ref[...].astype(jnp.float32)
    ids = jnp.concatenate(
        [ids, jnp.zeros((tokens, LANES - ids.shape[1]), jnp.float32)], axis=1
    )
    send_ref[:, feature:] = jnp.concatenate([ids, ids], axis=0).astype(jnp.bfloat16)


def fold(shared, residual, expert_ids):
    tokens, feature = residual.shape
    return pl.pallas_call(
        fold_kernel,
        out_shape=[
            jax.ShapeDtypeStruct((2 * tokens, feature), jnp.float32),
            jax.ShapeDtypeStruct((2 * tokens, feature + LANES), jnp.bfloat16),
        ],
        in_specs=[VMEM_SPEC] * 3,
        out_specs=[VMEM_SPEC] * 2,
        compiler_params=pltpu.CompilerParams(vmem_limit_bytes=4 << 20),
    )(place(shared), residual, expert_ids)


def placed_slots(ids, expert, step_in_block, block_rows):
    rows = ids.shape[0]
    row = lax.broadcasted_iota(jnp.int32, (rows, expert.shape[1]), 0)
    picked = jnp.zeros(row.shape, jnp.int32)
    for k in range(ids.shape[1]):
        picked = picked + jnp.where(ids[:, k : k + 1] == expert, 1, 0)
    before = jnp.zeros(row.shape, jnp.int32)
    for t in range(rows - 1):
        later = (row > t) & (row // block_rows == t // block_rows)
        before = before + jnp.where(later, picked[t : t + 1, :], 0)
    return (picked > 0) & (before == step_in_block)


def stream_kernel(
    part_ref,
    other_ref,
    gain_ref,
    ids_ref,
    share_ref,
    rows_ref,
    stream_ref,
    coefficient_ref,
    total_ref,
):
    rows, feature = part_ref.shape
    tokens = rows // 2
    members, zone_slots, _ = rows_ref.shape
    capacity = zone_slots // 2
    zone = own_zone()
    step = column_step(feature)
    blocks = [slice(k * step, (k + 1) * step) for k in range(feature // step)]
    square = jnp.zeros((rows, 1), jnp.float32)
    for columns in blocks:
        total = part_ref[:, columns] + other_ref[:, columns].astype(jnp.float32)
        total_ref[:, columns] = total
        stream_ref[:, columns] = jnp.where(zone == 0, total[:tokens], total[tokens:])
        square = square + jnp.sum(total * total, axis=1, keepdims=True)
    scale = lax.rsqrt(square / feature + norm_epsilon)

    own_ids = ids_ref[...].astype(jnp.float32)
    slots = coefficient_ref.shape[1]
    slot = lax.broadcasted_iota(jnp.int32, (tokens, slots), 1)
    expert = (slot // capacity).astype(jnp.float32)
    share = jnp.zeros((tokens, slots), jnp.float32)
    for k in range(ids_ref.shape[1]):
        share = share + jnp.where(own_ids[:, k : k + 1] == expert, share_ref[:, k : k + 1], 0.0)
    own_placed = placed_slots(own_ids, expert, slot % capacity, tokens)
    coefficient_ref[...] = jnp.where(own_placed, share, 0.0)

    width = -(-members * zone_slots // LANES) * LANES
    row = lax.broadcasted_iota(jnp.int32, (rows, 1), 0)
    other_ids = other_ref[:, feature : feature + ids_ref.shape[1]].astype(jnp.float32)
    ids = jnp.where(row // tokens == zone, jnp.concatenate([own_ids, own_ids], axis=0), other_ids)
    slot = lax.broadcasted_iota(jnp.int32, (rows, width), 1)
    expert = (zone * members + slot // zone_slots).astype(jnp.float32)
    placed = placed_slots(ids, expert, slot % capacity, tokens)
    placed = placed & (slot // capacity % 2 == row // tokens)
    chooser = jnp.transpose(jnp.where(placed, 1.0, 0.0))[: members * zone_slots]
    chooser = chooser.astype(jnp.bfloat16)
    for columns in blocks:
        gain = jnp.concatenate(
            [
                gain_ref[part : part + 1, :]
                for part in range(columns.start // LANES, columns.stop // LANES)
            ],
            axis=1,
        )
        normed = (total_ref[:, columns] * scale * gain).astype(jnp.bfloat16)
        chosen = jnp.dot(chooser, normed, preferred_element_type=jnp.float32)
        rows_ref[:, :, columns] = chosen.astype(jnp.bfloat16).reshape(members, zone_slots, step)


def route(part, other, gain, expert_ids, expert_weights, experts, capacity):
    rows, feature = part.shape
    tokens = rows // 2
    slots = -(-experts * capacity // LANES) * LANES
    return pl.pallas_call(
        stream_kernel,
        out_shape=[
            jax.ShapeDtypeStruct((experts // 2, 2 * capacity, feature), jnp.bfloat16),
            jax.ShapeDtypeStruct((tokens, feature), jnp.float32),
            jax.ShapeDtypeStruct((tokens, slots), jnp.float32),
        ],
        in_specs=[VMEM_SPEC] * 5,
        out_specs=[VMEM_SPEC] * 3,
        scratch_shapes=[pltpu.VMEM(part.shape, jnp.float32)],
        compiler_params=pltpu.CompilerParams(vmem_limit_bytes=4 << 20),
    )(
        place(part),
        place(other),
        gain.reshape(feature // LANES, LANES),
        expert_ids,
        expert_weights,
    )


def mix_kernel(returned_ref, coefficient_ref, stream_ref, out_ref):
    experts, capacity, feature = returned_ref.shape
    tokens = stream_ref.shape[0]
    count = experts * capacity
    rest = coefficient_ref[:, :count]
    terms = []
    for _ in range(3):
        term = rest.astype(jnp.bfloat16).astype(jnp.float32)
        rest = rest - term
        terms.append(term)
    terms.append(jnp.zeros_like(rest))
    weights = jnp.concatenate(terms, axis=0).astype(jnp.bfloat16)
    step = column_step(feature)
    for k in range(feature // step):
        columns = slice(k * step, (k + 1) * step)
        parts = jnp.dot(
            weights,
            returned_ref[:, :, columns].reshape(count, step),
            preferred_element_type=jnp.float32,
        )
        mixture = parts[:tokens] + parts[tokens : 2 * tokens] + parts[2 * tokens : 3 * tokens]
        out_ref[:, columns] = (stream_ref[:, columns] + mixture).astype(jnp.bfloat16)


def mix(returned, coefficient, stream):
    return pl.pallas_call(
        mix_kernel,
        out_shape=jax.ShapeDtypeStruct(stream.shape, jnp.bfloat16),
        in_specs=[VMEM_SPEC] * 3,
        out_specs=VMEM_SPEC,
        compiler_params=pltpu.CompilerParams(vmem_limit_bytes=4 << 20),
    )(place(returned), place(coefficient), place(stream))


def fill_hidden(rows, gate_ref, up_ref, hidden_ref):
    width = gate_ref.shape[1]
    step = 256 if width % 256 == 0 else width
    for k in range(width // step):
        columns = slice(k * step, (k + 1) * step)
        gate_part = jnp.dot(rows, gate_ref[:, columns], preferred_element_type=jnp.float32)
        up_part = jnp.dot(rows, up_ref[:, columns], preferred_element_type=jnp.float32)
        hidden_ref[:, columns] = (gate_part / (1.0 + jnp.exp(-gate_part)) * up_part).astype(
            jnp.bfloat16
        )


def fill_partial(hidden, down_ref, out_ref):
    step = column_step(down_ref.shape[1])
    for k in range(down_ref.shape[1] // step):
        columns = slice(k * step, (k + 1) * step)
        out_ref[:, columns] = jnp.dot(
            hidden, down_ref[:, columns], preferred_element_type=jnp.float32
        ).astype(jnp.bfloat16)


def own_hidden_kernel(rows_ref, gate_ref, up_ref, down_hbm, hidden_ref, down_ref, sem):
    load = pltpu.make_async_copy(down_hbm, down_ref, sem)
    load.start()
    shape = rows_ref.shape
    rows = rows_ref[...].reshape(shape[0] * shape[1], shape[2])
    fill_hidden(rows, gate_ref, up_ref, hidden_ref)
    load.wait()


def own_hidden(rows, gate, up, down):
    count = rows.shape[0] * rows.shape[1]
    return pl.pallas_call(
        own_hidden_kernel,
        out_shape=[
            jax.ShapeDtypeStruct((count, gate.shape[1]), jnp.bfloat16),
            pltpu.VMEM(down.shape, down.dtype),
        ],
        in_specs=[VMEM_SPEC] * 3 + [HBM_SPEC],
        out_specs=[VMEM_SPEC] * 2,
        scratch_shapes=[pltpu.SemaphoreType.DMA],
        compiler_params=pltpu.CompilerParams(vmem_limit_bytes=8 << 20),
        cost_estimate=pl.CostEstimate(
            flops=4 * count * gate.size, bytes_accessed=6 * gate.size, transcendentals=0
        ),
    )(place(rows), place(gate), place(up), stay(down))


def other_partial_kernel(rows_ref, gate_ref, up_ref, down_ref, send_ref, hidden_ref):
    shape = rows_ref.shape
    rows = rows_ref[...].reshape(shape[0] * shape[1], shape[2])
    fill_hidden(rows, gate_ref, up_ref, hidden_ref)
    fill_partial(hidden_ref[...], down_ref, send_ref)


def other_partial(rows, gate, up, down):
    count, feature = rows.shape[0] * rows.shape[1], rows.shape[2]
    return pl.pallas_call(
        other_partial_kernel,
        out_shape=jax.ShapeDtypeStruct((count, feature), jnp.bfloat16),
        in_specs=[VMEM_SPEC] * 4,
        out_specs=VMEM_SPEC,
        scratch_shapes=[pltpu.VMEM((count, gate.shape[1]), jnp.bfloat16)],
        compiler_params=pltpu.CompilerParams(vmem_limit_bytes=8 << 20),
    )(place(rows), place(gate), place(up), place(down))


def own_partial_kernel(hidden_ref, down_ref, keep_ref):
    fill_partial(hidden_ref[...], down_ref, keep_ref)


def own_partial(hidden, down):
    return pl.pallas_call(
        own_partial_kernel,
        out_shape=jax.ShapeDtypeStruct((hidden.shape[0], down.shape[1]), jnp.bfloat16),
        in_specs=[VMEM_SPEC] * 2,
        out_specs=VMEM_SPEC,
        compiler_params=pltpu.CompilerParams(vmem_limit_bytes=4 << 20),
        cost_estimate=pl.CostEstimate(
            flops=2 * hidden.shape[0] * down.size, bytes_accessed=2 * down.size, transcendentals=0
        ),
    )(place(hidden), place(down))


def swap_sides(block):
    return lax.ppermute(block, "side", [(0, 1), (1, 0)])


def local(
    queries,
    latent_cache,
    new_latent,
    lengths,
    residual,
    norm_gain,
    value_up,
    output_proj,
    expert_ids,
    expert_weights,
    gate_proj,
    up_proj,
    down_proj,
):
    row_count = queries.shape[0]
    feature = residual.shape[1]
    ep_count = lax.axis_size("ep")
    side_count = lax.axis_size("side")
    assert side_count == 2 and ep_count % 2 == 0 and ep_count <= 256
    flat_out = output_proj.reshape(output_proj.shape[0] * output_proj.shape[1], feature)
    capacity = min(
        row_count, max(2, (row_count * expert_ids.shape[1] + ep_count - 1) // ep_count)
    )

    latent, value_up, flat_out = attend(
        queries, latent_cache, new_latent, lengths, value_up, flat_out, ep_count * side_count
    )
    arrived = lax.all_to_all(latent, ("ep", "side"), split_axis=0, concat_axis=0, tiled=True)
    send, own_heads, gate = project_heads(arrived, value_up, flat_out, gate_proj[0])
    from_other = swap_sides(send)
    keep, up = project_own(own_heads, flat_out, up_proj[0])
    members = ep_count // 2
    zones = [list(range(members)), list(range(members, ep_count))]
    contribution = sum_halves(keep, from_other, members, 1)
    shared = lax.all_to_all(
        contribution, "ep", split_axis=0, concat_axis=0, tiled=True, axis_index_groups=zones
    )
    part, part_copy = fold(shared, residual, expert_ids)
    other_part = lax.ppermute(
        part_copy, "ep", [(e, (e + members) % ep_count) for e in range(ep_count)]
    )
    outbound, stream, coefficient = route(
        part, other_part, norm_gain, expert_ids, expert_weights, ep_count, capacity
    )
    own_rows = lax.all_to_all(
        outbound, "ep", split_axis=0, concat_axis=0, tiled=True, axis_index_groups=zones
    )
    other_rows = swap_sides(own_rows)
    hidden, down = own_hidden(own_rows, gate, up, down_proj[0])
    send = other_partial(other_rows, gate, up, down)
    other = swap_sides(send)
    keep = own_partial(hidden, down)
    both = sum_halves(keep, other, ep_count, 2)
    returned = lax.all_to_all(both, "ep", split_axis=0, concat_axis=0, tiled=True)
    return mix(returned, coefficient, stream)


def solution(mesh):
    in_specs = (
        P(("groups", "ep", "side"), None, None),
        P(("groups", "ep", "side"), None, None),
        P(("groups", "ep", "side"), None),
        P(("groups", "ep", "side")),
        P(("groups", "ep", "side"), None),
        P(),
        P(("ep", "side"), None, None),
        P(("ep", "side"), None, None),
        P(("groups", "ep", "side"), None),
        P(("groups", "ep", "side"), None),
        P("ep", None, "side"),
        P("ep", None, "side"),
        P("ep", "side", None),
    )
    out_specs = P(("groups", "ep", "side"), None)
    return jax.shard_map(local, mesh=mesh, in_specs=in_specs, out_specs=out_specs, check_vma=False)
```

```python
import functools

import jax
import jax.numpy as jnp
from jax import lax
from jax.experimental import pallas as pl
from jax.experimental.pallas import tpu as pltpu
from jax.sharding import PartitionSpec as P

LAT = 512
QKD = 192
LANES = 128


norm_epsilon = 1e-06
masked_score = -1e30

VMEM_SPEC = pl.BlockSpec(memory_space=pltpu.VMEM)
HBM_SPEC = pl.BlockSpec(memory_space=pltpu.HBM)


def stay(array):
    return pltpu.with_memory_space_constraint(array, pltpu.HBM)


def place(array):
    return pltpu.with_memory_space_constraint(array, pltpu.VMEM)


def column_step(width):
    for step in (512, 384, 256, 128):
        if width % step == 0:
            return step
    return width


def left_columns(width):
    step = column_step(width)
    return width // step * 3 // 4 * step


def attention_kernel(
    lengths_hbm,
    queries_hbm,
    cache_hbm,
    fresh_hbm,
    up_hbm,
    project_hbm,
    out_ref,
    up_ref,
    project_ref,
    lengths_ref,
    queries_ref,
    cache_ref,
    fresh_ref,
    sems,
):
    requests = cache_hbm.shape[0]
    positions = queries_hbm.shape[0] // requests
    first = [
        pltpu.make_async_copy(lengths_hbm, lengths_ref, sems.at[0]),
        pltpu.make_async_copy(fresh_hbm, fresh_ref, sems.at[1]),
    ]
    pieces = []
    for r in range(requests):
        tokens_of = pl.ds(r * positions, positions)
        pieces.append(
            [
                pltpu.make_async_copy(cache_hbm.at[r], cache_ref.at[r], sems.at[2 + 2 * r]),
                pltpu.make_async_copy(
                    queries_hbm.at[tokens_of], queries_ref.at[tokens_of], sems.at[3 + 2 * r]
                ),
            ]
        )
    count = 2 + 2 * requests
    loads = [
        pltpu.make_async_copy(up_hbm, up_ref, sems.at[count]),
        pltpu.make_async_copy(
            project_hbm.at[:, : project_ref.shape[1]], project_ref, sems.at[count + 1]
        ),
    ]
    for copy in first + sum(pieces, []) + loads:
        copy.start()
    factor = 1.0 / QKD**0.5
    context = cache_ref.shape[2]
    heads = queries_ref.shape[2]
    holders, block, latent_width = out_ref.shape
    rows = block // requests
    own_heads = rows // positions
    extra = 16
    width = positions * heads
    target = lax.broadcasted_iota(jnp.int32, (width, width), 0)
    source = lax.broadcasted_iota(jnp.int32, (width, width), 1)
    origin = (
        (target % rows) // own_heads * heads + target // rows * own_heads + target % own_heads
    )
    sorter = jnp.where(source == origin, 1.0, 0.0).astype(jnp.bfloat16)
    row = lax.broadcasted_iota(jnp.int32, (context + extra, width), 0)
    step = lax.broadcasted_iota(jnp.int32, (context + extra, width), 1) // heads
    fresh_live = (row >= context) & (row - context <= step)
    tail_row = lax.broadcasted_iota(jnp.int32, (extra, width), 0)
    key_row = lax.broadcasted_iota(jnp.int32, (context + extra, LANES), 0)
    scale_columns = jnp.where(
        (key_row >= context + positions) & (key_row < context + positions + 3), 1.0, 0.0
    ).astype(jnp.bfloat16)
    for copy in first + sum(pieces, []):
        copy.wait()
    for r in range(requests):
        fresh = fresh_ref[r * positions : (r + 1) * positions, :]
        keys = jnp.concatenate(
            [
                jnp.transpose(cache_ref[r]),
                fresh,
                jnp.zeros((extra - positions, fresh.shape[1]), fresh.dtype),
            ],
            axis=0,
        )
        wanted = jnp.concatenate(
            [queries_ref[r * positions + j] for j in range(positions)], axis=1
        )
        scores = jnp.dot(keys, wanted, preferred_element_type=jnp.float32) * factor
        live = (row < lengths_ref[r]) | fresh_live
        scores = jnp.where(live, scores, masked_score)
        highest = jnp.max(scores, axis=0, keepdims=True)
        weights = jnp.where(live, jnp.exp(scores - highest), 0.0)
        inverse = 1.0 / jnp.sum(weights, axis=0, keepdims=True)
        tail = weights[context:]
        for n in range(3):
            term = inverse.astype(jnp.bfloat16).astype(jnp.float32)
            inverse = inverse - term
            tail = jnp.where(tail_row == positions + n, term, tail)
        weights = jnp.concatenate([weights[:context], tail], axis=0).astype(jnp.bfloat16)
        ordered = lax.dot_general(
            sorter, weights, (((1,), (1,)), ((), ())), preferred_element_type=jnp.float32
        )
        ordered = ordered.astype(jnp.bfloat16)
        scale = jnp.dot(ordered, scale_columns, preferred_element_type=jnp.float32)
        merged = jnp.dot(ordered, keys[:, :latent_width], preferred_element_type=jnp.float32)
        for part in range(latent_width // LANES):
            columns = slice(part * LANES, (part + 1) * LANES)
            out_ref[:, r * rows : (r + 1) * rows, columns] = (
                (merged[:, columns] * scale).astype(jnp.bfloat16).reshape(holders, rows, LANES)
            )
    for copy in loads:
        copy.wait()


def attend(queries, latent_cache, new_latent, lengths, value_up, flat_out, holders):
    tokens, heads, _ = queries.shape
    requests = latent_cache.shape[0]
    block = tokens * heads // holders
    operands = (lengths, jnp.swapaxes(queries, 1, 2), jnp.swapaxes(latent_cache, 1, 2), new_latent)
    return pl.pallas_call(
        attention_kernel,
        out_shape=[
            jax.ShapeDtypeStruct((holders, block, LAT), jnp.bfloat16),
            pltpu.VMEM(value_up.shape, value_up.dtype),
            pltpu.VMEM((flat_out.shape[0], left_columns(flat_out.shape[1])), flat_out.dtype),
        ],
        in_specs=[HBM_SPEC] * 6,
        out_specs=[VMEM_SPEC] * 3,
        scratch_shapes=[pltpu.SMEM(lengths.shape, lengths.dtype)]
        + [pltpu.VMEM(x.shape, x.dtype) for x in operands[1:]]
        + [pltpu.SemaphoreType.DMA((4 + 2 * requests,))],
        compiler_params=pltpu.CompilerParams(vmem_limit_bytes=16 << 20),
    )(*map(stay, operands + (value_up, flat_out)))


def project_columns(rows, weight_ref, out_ref, start):
    step = column_step(weight_ref.shape[1])
    for k in range(weight_ref.shape[1] // step):
        out_ref[:, start + k * step : start + (k + 1) * step] = jnp.dot(
            rows, weight_ref[:, k * step : (k + 1) * step], preferred_element_type=jnp.float32
        ).astype(out_ref.dtype)


def head_kernel(
    arrived_ref, up_ref, left_ref, out_hbm, send_ref, own_ref, right_ref, sem
):
    load = pltpu.make_async_copy(out_hbm.at[:, left_ref.shape[1] :], right_ref, sem)
    load.start()
    tokens_in = arrived_ref.shape[1] // up_ref.shape[0]
    sources, block, latent_width = arrived_ref.shape
    own_heads, _, value_width = up_ref.shape
    rows = sources * tokens_in
    latent = arrived_ref[...].reshape(sources * block, latent_width)
    head = lax.broadcasted_iota(jnp.int32, (sources * block, value_width), 0) % own_heads
    outs = []
    for i in range(own_heads):
        out = jnp.dot(latent, up_ref[i], preferred_element_type=jnp.float32)
        outs.append(jnp.where(head == i, out, 0.0).astype(jnp.bfloat16))
    heads = jnp.concatenate(outs, axis=1)
    side = lax.axis_index("side")
    half = rows // 2
    target = lax.broadcasted_iota(jnp.int32, (rows, rows * own_heads), 0)
    source = lax.broadcasted_iota(jnp.int32, (rows, rows * own_heads), 1) // own_heads
    within = jnp.where(target < half, target, target - half)
    wanted_side = jnp.where(target < half, side, 1 - side)
    zone = (within // tokens_in) % 2
    member = within // (2 * tokens_in)
    chip = zone * (half // (2 * tokens_in)) + member
    origin = chip * (2 * tokens_in) + wanted_side * tokens_in + within % tokens_in
    sorter = jnp.where(source == origin, 1.0, 0.0).astype(jnp.bfloat16)
    ordered = jnp.dot(sorter, heads, preferred_element_type=jnp.float32).astype(jnp.bfloat16)
    own_ref[...] = ordered[:half]
    other = ordered[half:]
    project_columns(other, left_ref, send_ref, 0)
    load.wait()
    project_columns(other, right_ref, send_ref, left_ref.shape[1])


def project_heads(arrived, value_up, left, flat_out):
    sources, block, _ = arrived.shape
    own_heads, latent_width, value_width = value_up.shape
    half = sources * block // own_heads // 2
    depth, feature = flat_out.shape
    return pl.pallas_call(
        head_kernel,
        out_shape=[
            jax.ShapeDtypeStruct((half, feature), jnp.bfloat16),
            jax.ShapeDtypeStruct((half, own_heads * value_width), jnp.bfloat16),
            pltpu.VMEM((depth, feature - left.shape[1]), flat_out.dtype),
        ],
        in_specs=[VMEM_SPEC] * 3 + [HBM_SPEC],
        out_specs=[VMEM_SPEC] * 3,
        scratch_shapes=[pltpu.SemaphoreType.DMA],
        compiler_params=pltpu.CompilerParams(vmem_limit_bytes=16 << 20),
    )(place(arrived), place(value_up), place(left), stay(flat_out))


def own_kernel(heads_ref, left_ref, right_ref, keep_ref):
    heads = heads_ref[...]
    project_columns(heads, left_ref, keep_ref, 0)
    project_columns(heads, right_ref, keep_ref, left_ref.shape[1])


def project_own(heads, left, right):
    rows, feature = heads.shape[0], left.shape[1] + right.shape[1]
    size = heads.shape[1] * feature
    return pl.pallas_call(
        own_kernel,
        out_shape=jax.ShapeDtypeStruct((rows, feature), jnp.float32),
        in_specs=[VMEM_SPEC] * 3,
        out_specs=VMEM_SPEC,
        compiler_params=pltpu.CompilerParams(vmem_limit_bytes=4 << 20),
        cost_estimate=pl.CostEstimate(
            flops=2 * rows * size, bytes_accessed=2 * size, transcendentals=0
        ),
    )(place(heads), place(left), place(right))


def load_kernel(after_ref, gate_hbm, up_hbm, gate_ref, up_ref, sems):
    loads = [
        pltpu.make_async_copy(gate_hbm, gate_ref, sems.at[0]),
        pltpu.make_async_copy(up_hbm, up_ref, sems.at[1]),
    ]
    for copy in loads:
        copy.start()
    for copy in loads:
        copy.wait()


def load_weights(after, gate, up):
    return pl.pallas_call(
        load_kernel,
        out_shape=[pltpu.VMEM(gate.shape, gate.dtype), pltpu.VMEM(up.shape, up.dtype)],
        in_specs=[VMEM_SPEC] + [HBM_SPEC] * 2,
        out_specs=[VMEM_SPEC] * 2,
        scratch_shapes=[pltpu.SemaphoreType.DMA((2,))],
        compiler_params=pltpu.CompilerParams(vmem_limit_bytes=1 << 20),
        cost_estimate=pl.CostEstimate(
            flops=0, bytes_accessed=2 * (gate.size + up.size), transcendentals=0
        ),
    )(place(after), stay(gate), stay(up))


def sum_kernel(zones, keep_ref, other_ref, out_ref):
    groups, rows, feature = out_ref.shape
    members = groups // zones
    step = column_step(feature)
    for k in range(feature // step):
        columns = slice(k * step, (k + 1) * step)
        total = keep_ref[:, columns].astype(jnp.float32) + other_ref[:, columns].astype(
            jnp.float32
        )
        total = total.astype(jnp.bfloat16).reshape(groups, rows, step)
        if zones == 1:
            out_ref[:, :, columns] = total
        else:
            for group in range(groups):
                out_ref[group % zones * members + group // zones, :, columns] = total[group]


def sum_halves(keep, other, groups, zones):
    count, feature = keep.shape
    return pl.pallas_call(
        functools.partial(sum_kernel, zones),
        out_shape=jax.ShapeDtypeStruct((groups, count // groups, feature), jnp.bfloat16),
        in_specs=[VMEM_SPEC] * 2,
        out_specs=VMEM_SPEC,
        compiler_params=pltpu.CompilerParams(vmem_limit_bytes=4 << 20),
    )(place(keep), place(other))


def own_zone():
    return lax.axis_index("ep") // (lax.axis_size("ep") // 2)


def fold_kernel(shared_ref, residual_ref, ids_ref, part_ref, send_ref):
    tokens, feature = residual_ref.shape
    rows = 2 * tokens
    mine = lax.broadcasted_iota(jnp.int32, (rows, 1), 0) // tokens == own_zone()
    step = column_step(feature)
    for k in range(feature // step):
        columns = slice(k * step, (k + 1) * step)
        part = jnp.sum(shared_ref[:, :, columns].astype(jnp.float32), axis=0)
        residual = residual_ref[:, columns].astype(jnp.float32)
        part = part + jnp.where(mine, jnp.concatenate([residual, residual], axis=0), 0.0)
        part_ref[:, columns] = part
        send_ref[:, columns] = part.astype(jnp.bfloat16)
    ids = ids_ref[...].astype(jnp.float32)
    ids = jnp.concatenate(
        [ids, jnp.zeros((tokens, LANES - ids.shape[1]), jnp.float32)], axis=1
    )
    send_ref[:, feature:] = jnp.concatenate([ids, ids], axis=0).astype(jnp.bfloat16)


def fold(shared, residual, expert_ids):
    tokens, feature = residual.shape
    return pl.pallas_call(
        fold_kernel,
        out_shape=[
            jax.ShapeDtypeStruct((2 * tokens, feature), jnp.float32),
            jax.ShapeDtypeStruct((2 * tokens, feature + LANES), jnp.bfloat16),
        ],
        in_specs=[VMEM_SPEC] * 3,
        out_specs=[VMEM_SPEC] * 2,
        compiler_params=pltpu.CompilerParams(vmem_limit_bytes=4 << 20),
    )(place(shared), residual, expert_ids)


def placed_slots(ids, expert, step_in_block, block_rows):
    rows = ids.shape[0]
    row = lax.broadcasted_iota(jnp.int32, (rows, expert.shape[1]), 0)
    picked = jnp.zeros(row.shape, jnp.int32)
    for k in range(ids.shape[1]):
        picked = picked + jnp.where(ids[:, k : k + 1] == expert, 1, 0)
    before = jnp.zeros(row.shape, jnp.int32)
    for t in range(rows - 1):
        later = (row > t) & (row // block_rows == t // block_rows)
        before = before + jnp.where(later, picked[t : t + 1, :], 0)
    return (picked > 0) & (before == step_in_block)


def stream_kernel(
    part_ref,
    other_ref,
    gain_ref,
    ids_ref,
    share_ref,
    ready_ref,
    rows_ref,
    stream_ref,
    coefficient_ref,
    total_ref,
):
    rows, feature = part_ref.shape
    tokens = rows // 2
    members, zone_slots, _ = rows_ref.shape
    capacity = zone_slots // 2
    zone = own_zone()
    step = column_step(feature)
    blocks = [slice(k * step, (k + 1) * step) for k in range(feature // step)]
    square = jnp.zeros((rows, 1), jnp.float32)
    for columns in blocks:
        total = part_ref[:, columns] + other_ref[:, columns].astype(jnp.float32)
        total_ref[:, columns] = total
        stream_ref[:, columns] = jnp.where(zone == 0, total[:tokens], total[tokens:])
        square = square + jnp.sum(total * total, axis=1, keepdims=True)
    scale = lax.rsqrt(square / feature + norm_epsilon)

    own_ids = ids_ref[...].astype(jnp.float32)
    slots = coefficient_ref.shape[1]
    slot = lax.broadcasted_iota(jnp.int32, (tokens, slots), 1)
    expert = (slot // capacity).astype(jnp.float32)
    share = jnp.zeros((tokens, slots), jnp.float32)
    for k in range(ids_ref.shape[1]):
        share = share + jnp.where(own_ids[:, k : k + 1] == expert, share_ref[:, k : k + 1], 0.0)
    own_placed = placed_slots(own_ids, expert, slot % capacity, tokens)
    coefficient_ref[...] = jnp.where(own_placed, share, 0.0)

    width = -(-members * zone_slots // LANES) * LANES
    row = lax.broadcasted_iota(jnp.int32, (rows, 1), 0)
    other_ids = other_ref[:, feature : feature + ids_ref.shape[1]].astype(jnp.float32)
    ids = jnp.where(row // tokens == zone, jnp.concatenate([own_ids, own_ids], axis=0), other_ids)
    slot = lax.broadcasted_iota(jnp.int32, (rows, width), 1)
    expert = (zone * members + slot // zone_slots).astype(jnp.float32)
    placed = placed_slots(ids, expert, slot % capacity, tokens)
    placed = placed & (slot // capacity % 2 == row // tokens)
    chooser = jnp.transpose(jnp.where(placed, 1.0, 0.0))[: members * zone_slots]
    chooser = chooser.astype(jnp.bfloat16)
    for columns in blocks:
        gain = jnp.concatenate(
            [
                gain_ref[part : part + 1, :]
                for part in range(columns.start // LANES, columns.stop // LANES)
            ],
            axis=1,
        )
        normed = (total_ref[:, columns] * scale * gain).astype(jnp.bfloat16)
        chosen = jnp.dot(chooser, normed, preferred_element_type=jnp.float32)
        rows_ref[:, :, columns] = chosen.astype(jnp.bfloat16).reshape(members, zone_slots, step)


def route(part, other, gain, expert_ids, expert_weights, ready, experts, capacity):
    rows, feature = part.shape
    tokens = rows // 2
    slots = -(-experts * capacity // LANES) * LANES
    return pl.pallas_call(
        stream_kernel,
        out_shape=[
            jax.ShapeDtypeStruct((experts // 2, 2 * capacity, feature), jnp.bfloat16),
            jax.ShapeDtypeStruct((tokens, feature), jnp.float32),
            jax.ShapeDtypeStruct((tokens, slots), jnp.float32),
        ],
        in_specs=[VMEM_SPEC] * 6,
        out_specs=[VMEM_SPEC] * 3,
        scratch_shapes=[pltpu.VMEM(part.shape, jnp.float32)],
        compiler_params=pltpu.CompilerParams(vmem_limit_bytes=4 << 20),
    )(
        place(part),
        place(other),
        gain.reshape(feature // LANES, LANES),
        expert_ids,
        expert_weights,
        place(ready),
    )


def mix_kernel(returned_ref, coefficient_ref, stream_ref, out_ref):
    experts, capacity, feature = returned_ref.shape
    tokens = stream_ref.shape[0]
    count = experts * capacity
    rest = coefficient_ref[:, :count]
    terms = []
    for _ in range(3):
        term = rest.astype(jnp.bfloat16).astype(jnp.float32)
        rest = rest - term
        terms.append(term)
    terms.append(jnp.zeros_like(rest))
    weights = jnp.concatenate(terms, axis=0).astype(jnp.bfloat16)
    step = column_step(feature)
    for k in range(feature // step):
        columns = slice(k * step, (k + 1) * step)
        parts = jnp.dot(
            weights,
            returned_ref[:, :, columns].reshape(count, step),
            preferred_element_type=jnp.float32,
        )
        mixture = parts[:tokens] + parts[tokens : 2 * tokens] + parts[2 * tokens : 3 * tokens]
        out_ref[:, columns] = (stream_ref[:, columns] + mixture).astype(jnp.bfloat16)


def mix(returned, coefficient, stream):
    return pl.pallas_call(
        mix_kernel,
        out_shape=jax.ShapeDtypeStruct(stream.shape, jnp.bfloat16),
        in_specs=[VMEM_SPEC] * 3,
        out_specs=VMEM_SPEC,
        compiler_params=pltpu.CompilerParams(vmem_limit_bytes=4 << 20),
    )(place(returned), place(coefficient), place(stream))


def fill_hidden(rows, gate_ref, up_ref, hidden_ref):
    width = gate_ref.shape[1]
    step = 512 if width % 512 == 0 else width
    for k in range(width // step):
        columns = slice(k * step, (k + 1) * step)
        gate_part = jnp.dot(rows, gate_ref[:, columns], preferred_element_type=jnp.float32)
        up_part = jnp.dot(rows, up_ref[:, columns], preferred_element_type=jnp.float32)
        hidden_ref[:, columns] = (gate_part / (1.0 + jnp.exp(-gate_part)) * up_part).astype(
            jnp.bfloat16
        )


def fill_partial(hidden, top_ref, bottom_ref, out_ref):
    depth, feature = top_ref.shape
    step = column_step(feature)
    for k in range(feature // step):
        columns = slice(k * step, (k + 1) * step)
        out = jnp.dot(hidden[:, :depth], top_ref[:, columns], preferred_element_type=jnp.float32)
        out = out + jnp.dot(
            hidden[:, depth:], bottom_ref[:, columns], preferred_element_type=jnp.float32
        )
        out_ref[:, columns] = out.astype(jnp.bfloat16)


def own_hidden_kernel(rows_ref, gate_ref, up_ref, down_hbm, hidden_ref, top_ref, sem):
    load = pltpu.make_async_copy(down_hbm.at[pl.ds(0, top_ref.shape[0])], top_ref, sem)
    load.start()
    shape = rows_ref.shape
    rows = rows_ref[...].reshape(shape[0] * shape[1], shape[2])
    fill_hidden(rows, gate_ref, up_ref, hidden_ref)
    load.wait()


def own_hidden(rows, gate, up, down):
    count = rows.shape[0] * rows.shape[1]
    return pl.pallas_call(
        own_hidden_kernel,
        out_shape=[
            jax.ShapeDtypeStruct((count, gate.shape[1]), jnp.bfloat16),
            pltpu.VMEM((down.shape[0] // 2, down.shape[1]), down.dtype),
        ],
        in_specs=[VMEM_SPEC] * 3 + [HBM_SPEC],
        out_specs=[VMEM_SPEC] * 2,
        scratch_shapes=[pltpu.SemaphoreType.DMA],
        compiler_params=pltpu.CompilerParams(vmem_limit_bytes=8 << 20),
        cost_estimate=pl.CostEstimate(
            flops=4 * count * gate.size, bytes_accessed=5 * gate.size, transcendentals=0
        ),
    )(place(rows), place(gate), place(up), stay(down))


def other_partial_kernel(
    rows_ref, gate_ref, up_ref, top_ref, down_hbm, send_ref, bottom_ref, hidden_ref, sem
):
    depth = bottom_ref.shape[0]
    load = pltpu.make_async_copy(down_hbm.at[pl.ds(depth, depth)], bottom_ref, sem)
    load.start()
    shape = rows_ref.shape
    rows = rows_ref[...].reshape(shape[0] * shape[1], shape[2])
    fill_hidden(rows, gate_ref, up_ref, hidden_ref)
    load.wait()
    fill_partial(hidden_ref[...], top_ref, bottom_ref, send_ref)


def other_partial(rows, gate, up, top, down):
    count, feature = rows.shape[0] * rows.shape[1], rows.shape[2]
    return pl.pallas_call(
        other_partial_kernel,
        out_shape=[
            jax.ShapeDtypeStruct((count, feature), jnp.bfloat16),
            pltpu.VMEM(top.shape, top.dtype),
        ],
        in_specs=[VMEM_SPEC] * 4 + [HBM_SPEC],
        out_specs=[VMEM_SPEC] * 2,
        scratch_shapes=[
            pltpu.VMEM((count, gate.shape[1]), jnp.bfloat16),
            pltpu.SemaphoreType.DMA,
        ],
        compiler_params=pltpu.CompilerParams(vmem_limit_bytes=8 << 20),
    )(place(rows), place(gate), place(up), place(top), stay(down))


def own_partial_kernel(hidden_ref, top_ref, bottom_ref, keep_ref):
    fill_partial(hidden_ref[...], top_ref, bottom_ref, keep_ref)


def own_partial(hidden, top, bottom):
    rows, feature = hidden.shape[0], top.shape[1]
    return pl.pallas_call(
        own_partial_kernel,
        out_shape=jax.ShapeDtypeStruct((rows, feature), jnp.bfloat16),
        in_specs=[VMEM_SPEC] * 3,
        out_specs=VMEM_SPEC,
        compiler_params=pltpu.CompilerParams(vmem_limit_bytes=4 << 20),
        cost_estimate=pl.CostEstimate(
            flops=4 * rows * top.size, bytes_accessed=4 * top.size, transcendentals=0
        ),
    )(place(hidden), place(top), place(bottom))


def swap_sides(block):
    return lax.ppermute(block, "side", [(0, 1), (1, 0)])


def local(
    queries,
    latent_cache,
    new_latent,
    lengths,
    residual,
    norm_gain,
    value_up,
    output_proj,
    expert_ids,
    expert_weights,
    gate_proj,
    up_proj,
    down_proj,
):
    row_count = queries.shape[0]
    feature = residual.shape[1]
    ep_count = lax.axis_size("ep")
    side_count = lax.axis_size("side")
    assert side_count == 2 and ep_count % 2 == 0 and ep_count <= 256
    flat_out = output_proj.reshape(output_proj.shape[0] * output_proj.shape[1], feature)
    capacity = min(
        row_count, max(2, (row_count * expert_ids.shape[1] + ep_count - 1) // ep_count)
    )

    latent, value_up, left = attend(
        queries, latent_cache, new_latent, lengths, value_up, flat_out, ep_count * side_count
    )
    arrived = lax.all_to_all(latent, ("ep", "side"), split_axis=0, concat_axis=0, tiled=True)
    send, own_heads, right = project_heads(arrived, value_up, left, flat_out)
    from_other = swap_sides(send)
    keep = project_own(own_heads, left, right)
    members = ep_count // 2
    zones = [list(range(members)), list(range(members, ep_count))]
    contribution = sum_halves(keep, from_other, members, 1)
    shared = lax.all_to_all(
        contribution, "ep", split_axis=0, concat_axis=0, tiled=True, axis_index_groups=zones
    )
    part, part_copy = fold(shared, residual, expert_ids)
    other_part = lax.ppermute(
        part_copy, "ep", [(e, (e + members) % ep_count) for e in range(ep_count)]
    )
    gate, up = load_weights(part_copy, gate_proj[0], up_proj[0])
    outbound, stream, coefficient = route(
        part, other_part, norm_gain, expert_ids, expert_weights, gate, ep_count, capacity
    )
    own_rows = lax.all_to_all(
        outbound, "ep", split_axis=0, concat_axis=0, tiled=True, axis_index_groups=zones
    )
    other_rows = swap_sides(own_rows)
    hidden, top = own_hidden(own_rows, gate, up, down_proj[0])
    send, bottom = other_partial(other_rows, gate, up, top, down_proj[0])
    other = swap_sides(send)
    keep = own_partial(hidden, top, bottom)
    both = sum_halves(keep, other, ep_count, 2)
    returned = lax.all_to_all(both, "ep", split_axis=0, concat_axis=0, tiled=True)
    return mix(returned, coefficient, stream)


def solution(mesh):
    in_specs = (
        P(("groups", "ep", "side"), None, None),
        P(("groups", "ep", "side"), None, None),
        P(("groups", "ep", "side"), None),
        P(("groups", "ep", "side")),
        P(("groups", "ep", "side"), None),
        P(),
        P(("ep", "side"), None, None),
        P(("ep", "side"), None, None),
        P(("groups", "ep", "side"), None),
        P(("groups", "ep", "side"), None),
        P("ep", None, "side"),
        P("ep", None, "side"),
        P("ep", "side", None),
    )
    out_specs = P(("groups", "ep", "side"), None)
    return jax.shard_map(local, mesh=mesh, in_specs=in_specs, out_specs=out_specs, check_vma=False)
```

```python
import functools

import jax
import jax.numpy as jnp
from jax import lax
from jax.experimental import pallas as pl
from jax.experimental.pallas import tpu as pltpu
from jax.sharding import PartitionSpec as P

LAT = 512
QKD = 192
LANES = 128


norm_epsilon = 1e-06
masked_score = -1e30

VMEM_SPEC = pl.BlockSpec(memory_space=pltpu.VMEM)
HBM_SPEC = pl.BlockSpec(memory_space=pltpu.HBM)


def stay(array):
    return pltpu.with_memory_space_constraint(array, pltpu.HBM)


def place(array):
    return pltpu.with_memory_space_constraint(array, pltpu.VMEM)


def column_step(width):
    for step in (512, 384, 256, 128):
        if width % step == 0:
            return step
    return width


def left_columns(width):
    step = column_step(width)
    return width // step * 3 // 4 * step


def attention_kernel(
    lengths_hbm,
    queries_hbm,
    cache_hbm,
    fresh_hbm,
    up_hbm,
    project_hbm,
    out_ref,
    up_ref,
    project_ref,
    lengths_ref,
    queries_ref,
    cache_ref,
    fresh_ref,
    sems,
):
    requests = cache_hbm.shape[0]
    positions = queries_hbm.shape[0] // requests
    first = [
        pltpu.make_async_copy(lengths_hbm, lengths_ref, sems.at[0]),
        pltpu.make_async_copy(fresh_hbm, fresh_ref, sems.at[1]),
    ]
    pieces = []
    for r in range(requests):
        tokens_of = pl.ds(r * positions, positions)
        pieces.append(
            [
                pltpu.make_async_copy(cache_hbm.at[r], cache_ref.at[r], sems.at[2 + 2 * r]),
                pltpu.make_async_copy(
                    queries_hbm.at[tokens_of], queries_ref.at[tokens_of], sems.at[3 + 2 * r]
                ),
            ]
        )
    count = 2 + 2 * requests
    loads = [
        pltpu.make_async_copy(up_hbm, up_ref, sems.at[count]),
        pltpu.make_async_copy(
            project_hbm.at[:, : project_ref.shape[1]], project_ref, sems.at[count + 1]
        ),
    ]
    for copy in first + sum(pieces, []) + loads:
        copy.start()
    factor = 1.0 / QKD**0.5
    context = cache_ref.shape[2]
    heads = queries_ref.shape[2]
    holders, block, latent_width = out_ref.shape
    rows = block // requests
    own_heads = rows // positions
    extra = 16
    width = positions * heads
    target = lax.broadcasted_iota(jnp.int32, (width, width), 0)
    source = lax.broadcasted_iota(jnp.int32, (width, width), 1)
    origin = (
        (target % rows) // own_heads * heads + target // rows * own_heads + target % own_heads
    )
    sorter = jnp.where(source == origin, 1.0, 0.0).astype(jnp.bfloat16)
    row = lax.broadcasted_iota(jnp.int32, (context + extra, width), 0)
    step = lax.broadcasted_iota(jnp.int32, (context + extra, width), 1) // heads
    fresh_live = (row >= context) & (row - context <= step)
    tail_row = lax.broadcasted_iota(jnp.int32, (extra, width), 0)
    key_row = lax.broadcasted_iota(jnp.int32, (context + extra, LANES), 0)
    scale_columns = jnp.where(
        (key_row >= context + positions) & (key_row < context + positions + 3), 1.0, 0.0
    ).astype(jnp.bfloat16)
    for copy in first + sum(pieces, []):
        copy.wait()
    for r in range(requests):
        fresh = fresh_ref[r * positions : (r + 1) * positions, :]
        keys = jnp.concatenate(
            [
                jnp.transpose(cache_ref[r]),
                fresh,
                jnp.zeros((extra - positions, fresh.shape[1]), fresh.dtype),
            ],
            axis=0,
        )
        wanted = jnp.concatenate(
            [queries_ref[r * positions + j] for j in range(positions)], axis=1
        )
        scores = jnp.dot(keys, wanted, preferred_element_type=jnp.float32) * factor
        live = (row < lengths_ref[r]) | fresh_live
        scores = jnp.where(live, scores, masked_score)
        highest = jnp.max(scores, axis=0, keepdims=True)
        weights = jnp.exp(scores - highest)
        inverse = 1.0 / jnp.sum(weights, axis=0, keepdims=True)
        tail = weights[context:]
        for n in range(3):
            term = inverse.astype(jnp.bfloat16).astype(jnp.float32)
            inverse = inverse - term
            tail = jnp.where(tail_row == positions + n, term, tail)
        weights = jnp.concatenate([weights[:context], tail], axis=0).astype(jnp.bfloat16)
        ordered = lax.dot_general(
            sorter, weights, (((1,), (1,)), ((), ())), preferred_element_type=jnp.float32
        )
        ordered = ordered.astype(jnp.bfloat16)
        scale = jnp.dot(ordered, scale_columns, preferred_element_type=jnp.float32)
        merged = jnp.dot(ordered, keys[:, :latent_width], preferred_element_type=jnp.float32)
        for part in range(latent_width // LANES):
            columns = slice(part * LANES, (part + 1) * LANES)
            out_ref[:, r * rows : (r + 1) * rows, columns] = (
                (merged[:, columns] * scale).astype(jnp.bfloat16).reshape(holders, rows, LANES)
            )
    for copy in loads:
        copy.wait()


def attend(queries, latent_cache, new_latent, lengths, value_up, flat_out, holders):
    tokens, heads, _ = queries.shape
    requests = latent_cache.shape[0]
    block = tokens * heads // holders
    operands = (lengths, jnp.swapaxes(queries, 1, 2), jnp.swapaxes(latent_cache, 1, 2), new_latent)
    return pl.pallas_call(
        attention_kernel,
        out_shape=[
            jax.ShapeDtypeStruct((holders, block, LAT), jnp.bfloat16),
            pltpu.VMEM(value_up.shape, value_up.dtype),
            pltpu.VMEM((flat_out.shape[0], left_columns(flat_out.shape[1])), flat_out.dtype),
        ],
        in_specs=[HBM_SPEC] * 6,
        out_specs=[VMEM_SPEC] * 3,
        scratch_shapes=[pltpu.SMEM(lengths.shape, lengths.dtype)]
        + [pltpu.VMEM(x.shape, x.dtype) for x in operands[1:]]
        + [pltpu.SemaphoreType.DMA((4 + 2 * requests,))],
        compiler_params=pltpu.CompilerParams(vmem_limit_bytes=16 << 20),
    )(*map(stay, operands + (value_up, flat_out)))


def project_columns(rows, weight_ref, out_ref, start):
    step = column_step(weight_ref.shape[1])
    for k in range(weight_ref.shape[1] // step):
        out_ref[:, start + k * step : start + (k + 1) * step] = jnp.dot(
            rows, weight_ref[:, k * step : (k + 1) * step], preferred_element_type=jnp.float32
        ).astype(out_ref.dtype)


def head_kernel(
    arrived_ref, up_ref, left_ref, out_hbm, send_ref, own_ref, right_ref, sem
):
    load = pltpu.make_async_copy(out_hbm.at[:, left_ref.shape[1] :], right_ref, sem)
    load.start()
    tokens_in = arrived_ref.shape[1] // up_ref.shape[0]
    sources, block, latent_width = arrived_ref.shape
    own_heads, _, value_width = up_ref.shape
    rows = sources * tokens_in
    latent = arrived_ref[...].reshape(sources * block, latent_width)
    head = lax.broadcasted_iota(jnp.int32, (sources * block, value_width), 0) % own_heads
    outs = []
    for i in range(own_heads):
        out = jnp.dot(latent, up_ref[i], preferred_element_type=jnp.float32)
        outs.append(jnp.where(head == i, out, 0.0).astype(jnp.bfloat16))
    heads = jnp.concatenate(outs, axis=1)
    side = lax.axis_index("side")
    half = rows // 2
    target = lax.broadcasted_iota(jnp.int32, (rows, rows * own_heads), 0)
    source = lax.broadcasted_iota(jnp.int32, (rows, rows * own_heads), 1) // own_heads
    within = jnp.where(target < half, target, target - half)
    wanted_side = jnp.where(target < half, side, 1 - side)
    zone = (within // tokens_in) % 2
    member = within // (2 * tokens_in)
    chip = zone * (half // (2 * tokens_in)) + member
    origin = chip * (2 * tokens_in) + wanted_side * tokens_in + within % tokens_in
    sorter = jnp.where(source == origin, 1.0, 0.0).astype(jnp.bfloat16)
    ordered = jnp.dot(sorter, heads, preferred_element_type=jnp.float32).astype(jnp.bfloat16)
    own_ref[...] = ordered[:half]
    other = ordered[half:]
    project_columns(other, left_ref, send_ref, 0)
    load.wait()
    project_columns(other, right_ref, send_ref, left_ref.shape[1])


def project_heads(arrived, value_up, left, flat_out):
    sources, block, _ = arrived.shape
    own_heads, latent_width, value_width = value_up.shape
    half = sources * block // own_heads // 2
    depth, feature = flat_out.shape
    return pl.pallas_call(
        head_kernel,
        out_shape=[
            jax.ShapeDtypeStruct((half, feature), jnp.bfloat16),
            jax.ShapeDtypeStruct((half, own_heads * value_width), jnp.bfloat16),
            pltpu.VMEM((depth, feature - left.shape[1]), flat_out.dtype),
        ],
        in_specs=[VMEM_SPEC] * 3 + [HBM_SPEC],
        out_specs=[VMEM_SPEC] * 3,
        scratch_shapes=[pltpu.SemaphoreType.DMA],
        compiler_params=pltpu.CompilerParams(vmem_limit_bytes=16 << 20),
    )(place(arrived), place(value_up), place(left), stay(flat_out))


def own_kernel(heads_ref, left_ref, right_ref, keep_ref):
    heads = heads_ref[...]
    project_columns(heads, left_ref, keep_ref, 0)
    project_columns(heads, right_ref, keep_ref, left_ref.shape[1])


def project_own(heads, left, right):
    rows, feature = heads.shape[0], left.shape[1] + right.shape[1]
    size = heads.shape[1] * feature
    return pl.pallas_call(
        own_kernel,
        out_shape=jax.ShapeDtypeStruct((rows, feature), jnp.float32),
        in_specs=[VMEM_SPEC] * 3,
        out_specs=VMEM_SPEC,
        compiler_params=pltpu.CompilerParams(vmem_limit_bytes=4 << 20),
        cost_estimate=pl.CostEstimate(
            flops=2 * rows * size, bytes_accessed=2 * size, transcendentals=0
        ),
    )(place(heads), place(left), place(right))


def load_kernel(after_ref, gate_hbm, up_hbm, down_hbm, gate_ref, up_ref, top_ref, sems):
    loads = [
        pltpu.make_async_copy(gate_hbm, gate_ref, sems.at[0]),
        pltpu.make_async_copy(up_hbm, up_ref, sems.at[1]),
        pltpu.make_async_copy(down_hbm.at[pl.ds(0, top_ref.shape[0])], top_ref, sems.at[2]),
    ]
    for copy in loads:
        copy.start()
    for copy in loads:
        copy.wait()


def load_weights(after, gate, up, down):
    top = pltpu.VMEM((down.shape[0] // 2, down.shape[1]), down.dtype)
    return pl.pallas_call(
        load_kernel,
        out_shape=[pltpu.VMEM(gate.shape, gate.dtype), pltpu.VMEM(up.shape, up.dtype), top],
        in_specs=[VMEM_SPEC] + [HBM_SPEC] * 3,
        out_specs=[VMEM_SPEC] * 3,
        scratch_shapes=[pltpu.SemaphoreType.DMA((3,))],
        compiler_params=pltpu.CompilerParams(vmem_limit_bytes=1 << 20),
        cost_estimate=pl.CostEstimate(
            flops=0, bytes_accessed=2 * (gate.size + up.size + down.size // 2), transcendentals=0
        ),
    )(place(after), stay(gate), stay(up), stay(down))


def sum_kernel(zones, keep_ref, other_ref, out_ref):
    groups, rows, feature = out_ref.shape
    members = groups // zones
    step = column_step(feature)
    for k in range(feature // step):
        columns = slice(k * step, (k + 1) * step)
        total = keep_ref[:, columns].astype(jnp.float32) + other_ref[:, columns].astype(
            jnp.float32
        )
        total = total.astype(jnp.bfloat16).reshape(groups, rows, step)
        if zones == 1:
            out_ref[:, :, columns] = total
        else:
            for group in range(groups):
                out_ref[group % zones * members + group // zones, :, columns] = total[group]


def sum_halves(keep, other, groups, zones):
    count, feature = keep.shape
    return pl.pallas_call(
        functools.partial(sum_kernel, zones),
        out_shape=jax.ShapeDtypeStruct((groups, count // groups, feature), jnp.bfloat16),
        in_specs=[VMEM_SPEC] * 2,
        out_specs=VMEM_SPEC,
        compiler_params=pltpu.CompilerParams(vmem_limit_bytes=4 << 20),
    )(place(keep), place(other))


def own_zone():
    return lax.axis_index("ep") // (lax.axis_size("ep") // 2)


def fold_kernel(shared_ref, residual_ref, ids_ref, part_ref, send_ref):
    tokens, feature = residual_ref.shape
    rows = 2 * tokens
    mine = lax.broadcasted_iota(jnp.int32, (rows, 1), 0) // tokens == own_zone()
    step = column_step(feature)
    for k in range(feature // step):
        columns = slice(k * step, (k + 1) * step)
        part = jnp.sum(shared_ref[:, :, columns].astype(jnp.float32), axis=0)
        residual = residual_ref[:, columns].astype(jnp.float32)
        part = part + jnp.where(mine, jnp.concatenate([residual, residual], axis=0), 0.0)
        part_ref[:, columns] = part
        send_ref[:, columns] = part.astype(jnp.bfloat16)
    ids = ids_ref[...].astype(jnp.float32)
    ids = jnp.concatenate(
        [ids, jnp.zeros((tokens, LANES - ids.shape[1]), jnp.float32)], axis=1
    )
    send_ref[:, feature:] = jnp.concatenate([ids, ids], axis=0).astype(jnp.bfloat16)


def fold(shared, residual, expert_ids):
    tokens, feature = residual.shape
    return pl.pallas_call(
        fold_kernel,
        out_shape=[
            jax.ShapeDtypeStruct((2 * tokens, feature), jnp.float32),
            jax.ShapeDtypeStruct((2 * tokens, feature + LANES), jnp.bfloat16),
        ],
        in_specs=[VMEM_SPEC] * 3,
        out_specs=[VMEM_SPEC] * 2,
        compiler_params=pltpu.CompilerParams(vmem_limit_bytes=4 << 20),
    )(place(shared), residual, expert_ids)


def placed_slots(ids, expert, step_in_block, block_rows):
    rows = ids.shape[0]
    row = lax.broadcasted_iota(jnp.int32, (rows, expert.shape[1]), 0)
    picked = jnp.zeros(row.shape, jnp.int32)
    for k in range(ids.shape[1]):
        picked = picked + jnp.where(ids[:, k : k + 1] == expert, 1, 0)
    before = jnp.zeros(row.shape, jnp.int32)
    for t in range(rows - 1):
        later = (row > t) & (row // block_rows == t // block_rows)
        before = before + jnp.where(later, picked[t : t + 1, :], 0)
    return (picked > 0) & (before == step_in_block)


def stream_kernel(
    part_ref,
    other_ref,
    gain_ref,
    ids_ref,
    share_ref,
    ready_ref,
    rows_ref,
    stream_ref,
    coefficient_ref,
    total_ref,
):
    rows, feature = part_ref.shape
    tokens = rows // 2
    members, zone_slots, _ = rows_ref.shape
    capacity = zone_slots // 2
    zone = own_zone()
    step = column_step(feature)
    blocks = [slice(k * step, (k + 1) * step) for k in range(feature // step)]
    square = jnp.zeros((rows, 1), jnp.float32)
    for columns in blocks:
        total = part_ref[:, columns] + other_ref[:, columns].astype(jnp.float32)
        total_ref[:, columns] = total
        stream_ref[:, columns] = jnp.where(zone == 0, total[:tokens], total[tokens:])
        square = square + jnp.sum(total * total, axis=1, keepdims=True)
    scale = lax.rsqrt(square / feature + norm_epsilon)

    own_ids = ids_ref[...].astype(jnp.float32)
    slots = coefficient_ref.shape[1]
    slot = lax.broadcasted_iota(jnp.int32, (tokens, slots), 1)
    expert = (slot // capacity).astype(jnp.float32)
    share = jnp.zeros((tokens, slots), jnp.float32)
    for k in range(ids_ref.shape[1]):
        share = share + jnp.where(own_ids[:, k : k + 1] == expert, share_ref[:, k : k + 1], 0.0)
    own_placed = placed_slots(own_ids, expert, slot % capacity, tokens)
    coefficient_ref[...] = jnp.where(own_placed, share, 0.0)

    width = -(-members * zone_slots // LANES) * LANES
    row = lax.broadcasted_iota(jnp.int32, (rows, 1), 0)
    other_ids = other_ref[:, feature : feature + ids_ref.shape[1]].astype(jnp.float32)
    ids = jnp.where(row // tokens == zone, jnp.concatenate([own_ids, own_ids], axis=0), other_ids)
    slot = lax.broadcasted_iota(jnp.int32, (rows, width), 1)
    expert = (zone * members + slot // zone_slots).astype(jnp.float32)
    placed = placed_slots(ids, expert, slot % capacity, tokens)
    placed = placed & (slot // capacity % 2 == row // tokens)
    chooser = jnp.transpose(jnp.where(placed, 1.0, 0.0))[: members * zone_slots]
    chooser = chooser.astype(jnp.bfloat16)
    for columns in blocks:
        gain = jnp.concatenate(
            [
                gain_ref[part : part + 1, :]
                for part in range(columns.start // LANES, columns.stop // LANES)
            ],
            axis=1,
        )
        normed = (total_ref[:, columns] * scale * gain).astype(jnp.bfloat16)
        chosen = jnp.dot(chooser, normed, preferred_element_type=jnp.float32)
        rows_ref[:, :, columns] = chosen.astype(jnp.bfloat16).reshape(members, zone_slots, step)


def route(part, other, gain, expert_ids, expert_weights, ready, experts, capacity):
    rows, feature = part.shape
    tokens = rows // 2
    slots = -(-experts * capacity // LANES) * LANES
    return pl.pallas_call(
        stream_kernel,
        out_shape=[
            jax.ShapeDtypeStruct((experts // 2, 2 * capacity, feature), jnp.bfloat16),
            jax.ShapeDtypeStruct((tokens, feature), jnp.float32),
            jax.ShapeDtypeStruct((tokens, slots), jnp.float32),
        ],
        in_specs=[VMEM_SPEC] * 6,
        out_specs=[VMEM_SPEC] * 3,
        scratch_shapes=[pltpu.VMEM(part.shape, jnp.float32)],
        compiler_params=pltpu.CompilerParams(vmem_limit_bytes=4 << 20),
    )(
        place(part),
        place(other),
        gain.reshape(feature // LANES, LANES),
        expert_ids,
        expert_weights,
        place(ready),
    )


def mix_kernel(returned_ref, coefficient_ref, stream_ref, out_ref):
    experts, capacity, feature = returned_ref.shape
    tokens = stream_ref.shape[0]
    count = experts * capacity
    rest = coefficient_ref[:, :count]
    terms = []
    for _ in range(3):
        term = rest.astype(jnp.bfloat16).astype(jnp.float32)
        rest = rest - term
        terms.append(term)
    terms.append(jnp.zeros_like(rest))
    weights = jnp.concatenate(terms, axis=0).astype(jnp.bfloat16)
    step = column_step(feature)
    for k in range(feature // step):
        columns = slice(k * step, (k + 1) * step)
        parts = jnp.dot(
            weights,
            returned_ref[:, :, columns].reshape(count, step),
            preferred_element_type=jnp.float32,
        )
        mixture = parts[:tokens] + parts[tokens : 2 * tokens] + parts[2 * tokens : 3 * tokens]
        out_ref[:, columns] = (stream_ref[:, columns] + mixture).astype(jnp.bfloat16)


def mix(returned, coefficient, stream):
    return pl.pallas_call(
        mix_kernel,
        out_shape=jax.ShapeDtypeStruct(stream.shape, jnp.bfloat16),
        in_specs=[VMEM_SPEC] * 3,
        out_specs=VMEM_SPEC,
        compiler_params=pltpu.CompilerParams(vmem_limit_bytes=4 << 20),
    )(place(returned), place(coefficient), place(stream))


def fill_hidden(rows, gate_ref, up_ref, hidden_ref):
    width = gate_ref.shape[1]
    step = 512 if width % 512 == 0 else width
    for k in range(width // step):
        columns = slice(k * step, (k + 1) * step)
        gate_part = jnp.dot(rows, gate_ref[:, columns], preferred_element_type=jnp.float32)
        up_part = jnp.dot(rows, up_ref[:, columns], preferred_element_type=jnp.float32)
        hidden_ref[:, columns] = (gate_part / (1.0 + jnp.exp(-gate_part)) * up_part).astype(
            jnp.bfloat16
        )


def fill_partial(hidden, top_ref, bottom_ref, out_ref):
    depth, feature = top_ref.shape
    step = column_step(feature)
    for k in range(feature // step):
        columns = slice(k * step, (k + 1) * step)
        out = jnp.dot(hidden[:, :depth], top_ref[:, columns], preferred_element_type=jnp.float32)
        out = out + jnp.dot(
            hidden[:, depth:], bottom_ref[:, columns], preferred_element_type=jnp.float32
        )
        out_ref[:, columns] = out.astype(jnp.bfloat16)


def own_hidden_kernel(rows_ref, gate_ref, up_ref, down_hbm, hidden_ref, bottom_ref, sem):
    depth = bottom_ref.shape[0]
    load = pltpu.make_async_copy(
        down_hbm.at[pl.ds(down_hbm.shape[0] - depth, depth)], bottom_ref, sem
    )
    load.start()
    shape = rows_ref.shape
    rows = rows_ref[...].reshape(shape[0] * shape[1], shape[2])
    fill_hidden(rows, gate_ref, up_ref, hidden_ref)
    load.wait()


def own_hidden(rows, gate, up, down, top):
    count = rows.shape[0] * rows.shape[1]
    return pl.pallas_call(
        own_hidden_kernel,
        out_shape=[
            jax.ShapeDtypeStruct((count, gate.shape[1]), jnp.bfloat16),
            pltpu.VMEM((down.shape[0] - top.shape[0], down.shape[1]), down.dtype),
        ],
        in_specs=[VMEM_SPEC] * 3 + [HBM_SPEC],
        out_specs=[VMEM_SPEC] * 2,
        scratch_shapes=[pltpu.SemaphoreType.DMA],
        compiler_params=pltpu.CompilerParams(vmem_limit_bytes=8 << 20),
        cost_estimate=pl.CostEstimate(
            flops=4 * count * gate.size, bytes_accessed=5 * gate.size, transcendentals=0
        ),
    )(place(rows), place(gate), place(up), stay(down))


def other_partial_kernel(rows_ref, gate_ref, up_ref, top_ref, bottom_ref, send_ref, hidden_ref):
    shape = rows_ref.shape
    rows = rows_ref[...].reshape(shape[0] * shape[1], shape[2])
    fill_hidden(rows, gate_ref, up_ref, hidden_ref)
    fill_partial(hidden_ref[...], top_ref, bottom_ref, send_ref)


def other_partial(rows, gate, up, top, bottom):
    count, feature = rows.shape[0] * rows.shape[1], rows.shape[2]
    return pl.pallas_call(
        other_partial_kernel,
        out_shape=jax.ShapeDtypeStruct((count, feature), jnp.bfloat16),
        in_specs=[VMEM_SPEC] * 5,
        out_specs=VMEM_SPEC,
        scratch_shapes=[pltpu.VMEM((count, gate.shape[1]), jnp.bfloat16)],
        compiler_params=pltpu.CompilerParams(vmem_limit_bytes=8 << 20),
    )(place(rows), place(gate), place(up), place(top), place(bottom))


def own_partial_kernel(hidden_ref, top_ref, bottom_ref, keep_ref):
    fill_partial(hidden_ref[...], top_ref, bottom_ref, keep_ref)


def own_partial(hidden, top, bottom):
    rows, feature = hidden.shape[0], top.shape[1]
    return pl.pallas_call(
        own_partial_kernel,
        out_shape=jax.ShapeDtypeStruct((rows, feature), jnp.bfloat16),
        in_specs=[VMEM_SPEC] * 3,
        out_specs=VMEM_SPEC,
        compiler_params=pltpu.CompilerParams(vmem_limit_bytes=4 << 20),
        cost_estimate=pl.CostEstimate(
            flops=4 * rows * top.size, bytes_accessed=4 * top.size, transcendentals=0
        ),
    )(place(hidden), place(top), place(bottom))


def swap_sides(block):
    return lax.ppermute(block, "side", [(0, 1), (1, 0)])


def local(
    queries,
    latent_cache,
    new_latent,
    lengths,
    residual,
    norm_gain,
    value_up,
    output_proj,
    expert_ids,
    expert_weights,
    gate_proj,
    up_proj,
    down_proj,
):
    row_count = queries.shape[0]
    feature = residual.shape[1]
    ep_count = lax.axis_size("ep")
    side_count = lax.axis_size("side")
    assert side_count == 2 and ep_count % 2 == 0 and ep_count <= 256
    flat_out = output_proj.reshape(output_proj.shape[0] * output_proj.shape[1], feature)
    capacity = min(
        row_count, max(2, (row_count * expert_ids.shape[1] + ep_count - 1) // ep_count)
    )

    latent, value_up, left = attend(
        queries, latent_cache, new_latent, lengths, value_up, flat_out, ep_count * side_count
    )
    arrived = lax.all_to_all(latent, ("ep", "side"), split_axis=0, concat_axis=0, tiled=True)
    send, own_heads, right = project_heads(arrived, value_up, left, flat_out)
    from_other = swap_sides(send)
    keep = project_own(own_heads, left, right)
    members = ep_count // 2
    zones = [list(range(members)), list(range(members, ep_count))]
    contribution = sum_halves(keep, from_other, members, 1)
    shared = lax.all_to_all(
        contribution, "ep", split_axis=0, concat_axis=0, tiled=True, axis_index_groups=zones
    )
    part, part_copy = fold(shared, residual, expert_ids)
    other_part = lax.ppermute(
        part_copy, "ep", [(e, (e + members) % ep_count) for e in range(ep_count)]
    )
    gate, up, top = load_weights(part_copy, gate_proj[0], up_proj[0], down_proj[0])
    outbound, stream, coefficient = route(
        part, other_part, norm_gain, expert_ids, expert_weights, gate, ep_count, capacity
    )
    own_rows = lax.all_to_all(
        outbound, "ep", split_axis=0, concat_axis=0, tiled=True, axis_index_groups=zones
    )
    other_rows = swap_sides(own_rows)
    hidden, bottom = own_hidden(own_rows, gate, up, down_proj[0], top)
    send = other_partial(other_rows, gate, up, top, bottom)
    other = swap_sides(send)
    keep = own_partial(hidden, top, bottom)
    both = sum_halves(keep, other, ep_count, 2)
    returned = lax.all_to_all(both, "ep", split_axis=0, concat_axis=0, tiled=True)
    return mix(returned, coefficient, stream)


def solution(mesh):
    in_specs = (
        P(("groups", "ep", "side"), None, None),
        P(("groups", "ep", "side"), None, None),
        P(("groups", "ep", "side"), None),
        P(("groups", "ep", "side")),
        P(("groups", "ep", "side"), None),
        P(),
        P(("ep", "side"), None, None),
        P(("ep", "side"), None, None),
        P(("groups", "ep", "side"), None),
        P(("groups", "ep", "side"), None),
        P("ep", None, "side"),
        P("ep", None, "side"),
        P("ep", "side", None),
    )
    out_specs = P(("groups", "ep", "side"), None)
    return jax.shard_map(local, mesh=mesh, in_specs=in_specs, out_specs=out_specs, check_vma=False)
```

```python
import functools

import jax
import jax.numpy as jnp
from jax import lax
from jax.experimental import pallas as pl
from jax.experimental.pallas import tpu as pltpu
from jax.sharding import PartitionSpec as P

LAT = 512
QKD = 192
LANES = 128


norm_epsilon = 1e-06
masked_score = -1e30

VMEM_SPEC = pl.BlockSpec(memory_space=pltpu.VMEM)
HBM_SPEC = pl.BlockSpec(memory_space=pltpu.HBM)


def stay(array):
    return pltpu.with_memory_space_constraint(array, pltpu.HBM)


def place(array):
    return pltpu.with_memory_space_constraint(array, pltpu.VMEM)


def column_step(width):
    for step in (512, 384, 256, 128):
        if width % step == 0:
            return step
    return width


def left_columns(width):
    step = column_step(width)
    return width // step * 3 // 4 * step


def attention_kernel(
    lengths_hbm,
    queries_hbm,
    cache_hbm,
    fresh_hbm,
    up_hbm,
    project_hbm,
    out_ref,
    up_ref,
    project_ref,
    lengths_ref,
    queries_ref,
    cache_ref,
    fresh_ref,
    sems,
):
    requests = cache_hbm.shape[0]
    positions = queries_hbm.shape[0] // requests
    first = [
        pltpu.make_async_copy(lengths_hbm, lengths_ref, sems.at[0]),
        pltpu.make_async_copy(fresh_hbm, fresh_ref, sems.at[1]),
    ]
    pieces = []
    for r in range(requests):
        tokens_of = pl.ds(r * positions, positions)
        pieces.append(
            [
                pltpu.make_async_copy(cache_hbm.at[r], cache_ref.at[r], sems.at[2 + 2 * r]),
                pltpu.make_async_copy(
                    queries_hbm.at[tokens_of], queries_ref.at[tokens_of], sems.at[3 + 2 * r]
                ),
            ]
        )
    count = 2 + 2 * requests
    loads = [
        pltpu.make_async_copy(up_hbm, up_ref, sems.at[count]),
        pltpu.make_async_copy(
            project_hbm.at[:, : project_ref.shape[1]], project_ref, sems.at[count + 1]
        ),
    ]
    for copy in first + sum(pieces, []) + loads:
        copy.start()
    factor = 1.0 / QKD**0.5
    context = cache_ref.shape[2]
    heads = queries_ref.shape[2]
    holders, block, latent_width = out_ref.shape
    rows = block // requests
    own_heads = rows // positions
    extra = 16
    width = positions * heads
    target = lax.broadcasted_iota(jnp.int32, (width, width), 0)
    source = lax.broadcasted_iota(jnp.int32, (width, width), 1)
    origin = (
        (target % rows) // own_heads * heads + target // rows * own_heads + target % own_heads
    )
    sorter = jnp.where(source == origin, 1.0, 0.0).astype(jnp.bfloat16)
    row = lax.broadcasted_iota(jnp.int32, (context + extra, width), 0)
    step = lax.broadcasted_iota(jnp.int32, (context + extra, width), 1) // heads
    fresh_live = (row >= context) & (row - context <= step)
    tail_row = lax.broadcasted_iota(jnp.int32, (extra, width), 0)
    key_row = lax.broadcasted_iota(jnp.int32, (context + extra, LANES), 0)
    scale_columns = jnp.where(
        (key_row >= context + positions) & (key_row < context + positions + 3), 1.0, 0.0
    ).astype(jnp.bfloat16)
    for copy in first + sum(pieces, []):
        copy.wait()
    for r in range(requests):
        fresh = fresh_ref[r * positions : (r + 1) * positions, :]
        keys = jnp.concatenate(
            [
                jnp.transpose(cache_ref[r]),
                fresh,
                jnp.zeros((extra - positions, fresh.shape[1]), fresh.dtype),
            ],
            axis=0,
        )
        wanted = jnp.concatenate(
            [queries_ref[r * positions + j] for j in range(positions)], axis=1
        )
        scores = jnp.dot(keys, wanted, preferred_element_type=jnp.float32) * factor
        live = (row < lengths_ref[r]) | fresh_live
        scores = jnp.where(live, scores, masked_score)
        highest = jnp.max(scores, axis=0, keepdims=True)
        weights = jnp.exp(scores - highest)
        inverse = 1.0 / jnp.sum(weights, axis=0, keepdims=True)
        tail = weights[context:]
        for n in range(3):
            term = inverse.astype(jnp.bfloat16).astype(jnp.float32)
            inverse = inverse - term
            tail = jnp.where(tail_row == positions + n, term, tail)
        weights = jnp.concatenate([weights[:context], tail], axis=0).astype(jnp.bfloat16)
        ordered = lax.dot_general(
            sorter, weights, (((1,), (1,)), ((), ())), preferred_element_type=jnp.float32
        )
        ordered = ordered.astype(jnp.bfloat16)
        scale = jnp.dot(ordered, scale_columns, preferred_element_type=jnp.float32)
        merged = jnp.dot(ordered, keys[:, :latent_width], preferred_element_type=jnp.float32)
        for part in range(latent_width // LANES):
            columns = slice(part * LANES, (part + 1) * LANES)
            out_ref[:, r * rows : (r + 1) * rows, columns] = (
                (merged[:, columns] * scale).astype(jnp.bfloat16).reshape(holders, rows, LANES)
            )
    for copy in loads:
        copy.wait()


def attend(queries, latent_cache, new_latent, lengths, value_up, flat_out, holders):
    tokens, heads, _ = queries.shape
    requests = latent_cache.shape[0]
    block = tokens * heads // holders
    operands = (lengths, jnp.swapaxes(queries, 1, 2), jnp.swapaxes(latent_cache, 1, 2), new_latent)
    return pl.pallas_call(
        attention_kernel,
        out_shape=[
            jax.ShapeDtypeStruct((holders, block, LAT), jnp.bfloat16),
            pltpu.VMEM(value_up.shape, value_up.dtype),
            pltpu.VMEM((flat_out.shape[0], left_columns(flat_out.shape[1])), flat_out.dtype),
        ],
        in_specs=[HBM_SPEC] * 6,
        out_specs=[VMEM_SPEC] * 3,
        scratch_shapes=[pltpu.SMEM(lengths.shape, lengths.dtype)]
        + [pltpu.VMEM(x.shape, x.dtype) for x in operands[1:]]
        + [pltpu.SemaphoreType.DMA((4 + 2 * requests,))],
        compiler_params=pltpu.CompilerParams(vmem_limit_bytes=16 << 20),
    )(*map(stay, operands + (value_up, flat_out)))


def project_columns(rows, weight_ref, out_ref, start):
    step = column_step(weight_ref.shape[1])
    for k in range(weight_ref.shape[1] // step):
        out_ref[:, start + k * step : start + (k + 1) * step] = jnp.dot(
            rows, weight_ref[:, k * step : (k + 1) * step], preferred_element_type=jnp.float32
        ).astype(out_ref.dtype)


def head_kernel(
    arrived_ref, up_ref, left_ref, out_hbm, send_ref, own_ref, right_ref, sem
):
    load = pltpu.make_async_copy(out_hbm.at[:, left_ref.shape[1] :], right_ref, sem)
    load.start()
    tokens_in = arrived_ref.shape[1] // up_ref.shape[0]
    sources, block, latent_width = arrived_ref.shape
    own_heads, _, value_width = up_ref.shape
    rows = sources * tokens_in
    latent = arrived_ref[...].reshape(sources * block, latent_width)
    if 8 % own_heads == 0 and sources * block % 8 == 0:
        head = lax.rem(lax.broadcasted_iota(jnp.int32, (8, value_width), 0), own_heads)
        head = jnp.concatenate([head] * (sources * block // 8), axis=0)
    else:
        head = lax.broadcasted_iota(jnp.int32, (sources * block, value_width), 0) % own_heads
    outs = []
    for i in range(own_heads):
        out = jnp.dot(latent, up_ref[i], preferred_element_type=jnp.float32)
        outs.append(jnp.where(head == i, out, 0.0).astype(jnp.bfloat16))
    heads = jnp.concatenate(outs, axis=1)
    side = lax.axis_index("side")
    half = rows // 2
    target = lax.broadcasted_iota(jnp.int32, (rows, LANES), 0)
    source = lax.broadcasted_iota(jnp.int32, (8, rows * own_heads), 1) // own_heads
    source = jnp.concatenate([source] * (rows // 8), axis=0)
    within = jnp.where(target < half, target, target - half)
    wanted_side = jnp.where(target < half, side, 1 - side)
    zone = (within // tokens_in) % 2
    member = within // (2 * tokens_in)
    chip = zone * (half // (2 * tokens_in)) + member
    origin = chip * (2 * tokens_in) + wanted_side * tokens_in + within % tokens_in
    origin = jnp.concatenate([origin] * (rows * own_heads // LANES), axis=1)
    sorter = jnp.where(source == origin, 1.0, 0.0).astype(jnp.bfloat16)
    ordered = jnp.dot(sorter, heads, preferred_element_type=jnp.float32).astype(jnp.bfloat16)
    own_ref[...] = ordered[:half]
    other = ordered[half:]
    project_columns(other, left_ref, send_ref, 0)
    load.wait()
    project_columns(other, right_ref, send_ref, left_ref.shape[1])


def project_heads(arrived, value_up, left, flat_out):
    sources, block, _ = arrived.shape
    own_heads, latent_width, value_width = value_up.shape
    half = sources * block // own_heads // 2
    depth, feature = flat_out.shape
    return pl.pallas_call(
        head_kernel,
        out_shape=[
            jax.ShapeDtypeStruct((half, feature), jnp.bfloat16),
            jax.ShapeDtypeStruct((half, own_heads * value_width), jnp.bfloat16),
            pltpu.VMEM((depth, feature - left.shape[1]), flat_out.dtype),
        ],
        in_specs=[VMEM_SPEC] * 3 + [HBM_SPEC],
        out_specs=[VMEM_SPEC] * 3,
        scratch_shapes=[pltpu.SemaphoreType.DMA],
        compiler_params=pltpu.CompilerParams(vmem_limit_bytes=16 << 20),
    )(place(arrived), place(value_up), place(left), stay(flat_out))


def own_kernel(heads_ref, left_ref, right_ref, keep_ref):
    heads = heads_ref[...]
    project_columns(heads, left_ref, keep_ref, 0)
    project_columns(heads, right_ref, keep_ref, left_ref.shape[1])


def project_own(heads, left, right):
    rows, feature = heads.shape[0], left.shape[1] + right.shape[1]
    size = heads.shape[1] * feature
    return pl.pallas_call(
        own_kernel,
        out_shape=jax.ShapeDtypeStruct((rows, feature), jnp.float32),
        in_specs=[VMEM_SPEC] * 3,
        out_specs=VMEM_SPEC,
        compiler_params=pltpu.CompilerParams(vmem_limit_bytes=4 << 20),
        cost_estimate=pl.CostEstimate(
            flops=2 * rows * size, bytes_accessed=2 * size, transcendentals=0
        ),
    )(place(heads), place(left), place(right))


def load_kernel(after_ref, gate_hbm, up_hbm, down_hbm, gate_ref, up_ref, top_ref, sems):
    loads = [
        pltpu.make_async_copy(gate_hbm, gate_ref, sems.at[0]),
        pltpu.make_async_copy(up_hbm, up_ref, sems.at[1]),
        pltpu.make_async_copy(down_hbm.at[pl.ds(0, top_ref.shape[0])], top_ref, sems.at[2]),
    ]
    for copy in loads:
        copy.start()
    for copy in loads:
        copy.wait()


def load_weights(after, gate, up, down):
    top = pltpu.VMEM((down.shape[0] // 2, down.shape[1]), down.dtype)
    return pl.pallas_call(
        load_kernel,
        out_shape=[pltpu.VMEM(gate.shape, gate.dtype), pltpu.VMEM(up.shape, up.dtype), top],
        in_specs=[VMEM_SPEC] + [HBM_SPEC] * 3,
        out_specs=[VMEM_SPEC] * 3,
        scratch_shapes=[pltpu.SemaphoreType.DMA((3,))],
        compiler_params=pltpu.CompilerParams(vmem_limit_bytes=1 << 20),
        cost_estimate=pl.CostEstimate(
            flops=0, bytes_accessed=2 * (gate.size + up.size + down.size // 2), transcendentals=0
        ),
    )(place(after), stay(gate), stay(up), stay(down))


def sum_kernel(zones, keep_ref, other_ref, out_ref):
    groups, rows, feature = out_ref.shape
    members = groups // zones
    step = column_step(feature)
    for k in range(feature // step):
        columns = slice(k * step, (k + 1) * step)
        total = keep_ref[:, columns].astype(jnp.float32) + other_ref[:, columns].astype(
            jnp.float32
        )
        total = total.astype(jnp.bfloat16).reshape(groups, rows, step)
        if zones == 1:
            out_ref[:, :, columns] = total
        else:
            for group in range(groups):
                out_ref[group % zones * members + group // zones, :, columns] = total[group]


def sum_halves(keep, other, groups, zones):
    count, feature = keep.shape
    return pl.pallas_call(
        functools.partial(sum_kernel, zones),
        out_shape=jax.ShapeDtypeStruct((groups, count // groups, feature), jnp.bfloat16),
        in_specs=[VMEM_SPEC] * 2,
        out_specs=VMEM_SPEC,
        compiler_params=pltpu.CompilerParams(vmem_limit_bytes=4 << 20),
    )(place(keep), place(other))


def own_zone():
    return lax.axis_index("ep") // (lax.axis_size("ep") // 2)


def fold_kernel(shared_ref, residual_ref, ids_ref, part_ref, send_ref):
    tokens, feature = residual_ref.shape
    rows = 2 * tokens
    mine = lax.broadcasted_iota(jnp.int32, (rows, 1), 0) // tokens == own_zone()
    step = column_step(feature)
    for k in range(feature // step):
        columns = slice(k * step, (k + 1) * step)
        part = jnp.sum(shared_ref[:, :, columns].astype(jnp.float32), axis=0)
        residual = residual_ref[:, columns].astype(jnp.float32)
        part = part + jnp.where(mine, jnp.concatenate([residual, residual], axis=0), 0.0)
        part_ref[:, columns] = part
        send_ref[:, columns] = part.astype(jnp.bfloat16)
    ids = ids_ref[...].astype(jnp.float32)
    ids = jnp.concatenate(
        [ids, jnp.zeros((tokens, LANES - ids.shape[1]), jnp.float32)], axis=1
    )
    send_ref[:, feature:] = jnp.concatenate([ids, ids], axis=0).astype(jnp.bfloat16)


def fold(shared, residual, expert_ids):
    tokens, feature = residual.shape
    return pl.pallas_call(
        fold_kernel,
        out_shape=[
            jax.ShapeDtypeStruct((2 * tokens, feature), jnp.float32),
            jax.ShapeDtypeStruct((2 * tokens, feature + LANES), jnp.bfloat16),
        ],
        in_specs=[VMEM_SPEC] * 3,
        out_specs=[VMEM_SPEC] * 2,
        compiler_params=pltpu.CompilerParams(vmem_limit_bytes=4 << 20),
    )(place(shared), residual, expert_ids)


def placed_slots(ids, expert, step_in_block, block_rows):
    rows = ids.shape[0]
    row = lax.broadcasted_iota(jnp.int32, (rows, expert.shape[1]), 0)
    picked = jnp.zeros(row.shape, jnp.int32)
    for k in range(ids.shape[1]):
        picked = picked + jnp.where(ids[:, k : k + 1] == expert, 1, 0)
    before = jnp.zeros(row.shape, jnp.int32)
    for t in range(rows - 1):
        later = (row > t) & (row // block_rows == t // block_rows)
        before = before + jnp.where(later, picked[t : t + 1, :], 0)
    return (picked > 0) & (before == step_in_block)


def stream_kernel(
    part_ref,
    other_ref,
    gain_ref,
    ids_ref,
    share_ref,
    ready_ref,
    rows_ref,
    stream_ref,
    coefficient_ref,
    total_ref,
):
    rows, feature = part_ref.shape
    tokens = rows // 2
    members, zone_slots, _ = rows_ref.shape
    capacity = zone_slots // 2
    zone = own_zone()
    step = column_step(feature)
    blocks = [slice(k * step, (k + 1) * step) for k in range(feature // step)]
    square = jnp.zeros((rows, 1), jnp.float32)
    for columns in blocks:
        total = part_ref[:, columns] + other_ref[:, columns].astype(jnp.float32)
        total_ref[:, columns] = total
        stream_ref[:, columns] = jnp.where(zone == 0, total[:tokens], total[tokens:])
        square = square + jnp.sum(total * total, axis=1, keepdims=True)
    scale = lax.rsqrt(square / feature + norm_epsilon)

    own_ids = ids_ref[...].astype(jnp.float32)
    slots = coefficient_ref.shape[1]
    slot = lax.broadcasted_iota(jnp.int32, (tokens, slots), 1)
    expert = (slot // capacity).astype(jnp.float32)
    share = jnp.zeros((tokens, slots), jnp.float32)
    for k in range(ids_ref.shape[1]):
        share = share + jnp.where(own_ids[:, k : k + 1] == expert, share_ref[:, k : k + 1], 0.0)
    own_placed = placed_slots(own_ids, expert, slot % capacity, tokens)
    coefficient_ref[...] = jnp.where(own_placed, share, 0.0)

    width = -(-members * zone_slots // LANES) * LANES
    row = lax.broadcasted_iota(jnp.int32, (rows, 1), 0)
    other_ids = other_ref[:, feature : feature + ids_ref.shape[1]].astype(jnp.float32)
    ids = jnp.where(row // tokens == zone, jnp.concatenate([own_ids, own_ids], axis=0), other_ids)
    slot = lax.broadcasted_iota(jnp.int32, (rows, width), 1)
    expert = (zone * members + slot // zone_slots).astype(jnp.float32)
    placed = placed_slots(ids, expert, slot % capacity, tokens)
    placed = placed & (slot // capacity % 2 == row // tokens)
    chooser = jnp.transpose(jnp.where(placed, 1.0, 0.0))[: members * zone_slots]
    chooser = chooser.astype(jnp.bfloat16)
    for columns in blocks:
        gain = jnp.concatenate(
            [
                gain_ref[part : part + 1, :]
                for part in range(columns.start // LANES, columns.stop // LANES)
            ],
            axis=1,
        )
        normed = (total_ref[:, columns] * scale * gain).astype(jnp.bfloat16)
        chosen = jnp.dot(chooser, normed, preferred_element_type=jnp.float32)
        rows_ref[:, :, columns] = chosen.astype(jnp.bfloat16).reshape(members, zone_slots, step)


def route(part, other, gain, expert_ids, expert_weights, ready, experts, capacity):
    rows, feature = part.shape
    tokens = rows // 2
    slots = -(-experts * capacity // LANES) * LANES
    return pl.pallas_call(
        stream_kernel,
        out_shape=[
            jax.ShapeDtypeStruct((experts // 2, 2 * capacity, feature), jnp.bfloat16),
            jax.ShapeDtypeStruct((tokens, feature), jnp.float32),
            jax.ShapeDtypeStruct((tokens, slots), jnp.float32),
        ],
        in_specs=[VMEM_SPEC] * 6,
        out_specs=[VMEM_SPEC] * 3,
        scratch_shapes=[pltpu.VMEM(part.shape, jnp.float32)],
        compiler_params=pltpu.CompilerParams(vmem_limit_bytes=4 << 20),
    )(
        place(part),
        place(other),
        gain.reshape(feature // LANES, LANES),
        expert_ids,
        expert_weights,
        place(ready),
    )


def mix_kernel(returned_ref, coefficient_ref, stream_ref, out_ref):
    experts, capacity, feature = returned_ref.shape
    tokens = stream_ref.shape[0]
    count = experts * capacity
    rest = coefficient_ref[:, :count]
    terms = []
    for _ in range(3):
        term = rest.astype(jnp.bfloat16).astype(jnp.float32)
        rest = rest - term
        terms.append(term)
    terms.append(jnp.zeros_like(rest))
    weights = jnp.concatenate(terms, axis=0).astype(jnp.bfloat16)
    step = column_step(feature)
    for k in range(feature // step):
        columns = slice(k * step, (k + 1) * step)
        parts = jnp.dot(
            weights,
            returned_ref[:, :, columns].reshape(count, step),
            preferred_element_type=jnp.float32,
        )
        mixture = parts[:tokens] + parts[tokens : 2 * tokens] + parts[2 * tokens : 3 * tokens]
        out_ref[:, columns] = (stream_ref[:, columns] + mixture).astype(jnp.bfloat16)


def mix(returned, coefficient, stream):
    return pl.pallas_call(
        mix_kernel,
        out_shape=jax.ShapeDtypeStruct(stream.shape, jnp.bfloat16),
        in_specs=[VMEM_SPEC] * 3,
        out_specs=VMEM_SPEC,
        compiler_params=pltpu.CompilerParams(vmem_limit_bytes=4 << 20),
    )(place(returned), place(coefficient), place(stream))


def fill_hidden(rows, gate_ref, up_ref, hidden_ref):
    width = gate_ref.shape[1]
    step = 512 if width % 512 == 0 else width
    for k in range(width // step):
        columns = slice(k * step, (k + 1) * step)
        gate_part = jnp.dot(rows, gate_ref[:, columns], preferred_element_type=jnp.float32)
        up_part = jnp.dot(rows, up_ref[:, columns], preferred_element_type=jnp.float32)
        hidden_ref[:, columns] = (gate_part / (1.0 + jnp.exp(-gate_part)) * up_part).astype(
            jnp.bfloat16
        )


def fill_partial(hidden, top_ref, bottom_ref, out_ref):
    depth, feature = top_ref.shape
    step = column_step(feature)
    for k in range(feature // step):
        columns = slice(k * step, (k + 1) * step)
        out = jnp.dot(hidden[:, :depth], top_ref[:, columns], preferred_element_type=jnp.float32)
        out = out + jnp.dot(
            hidden[:, depth:], bottom_ref[:, columns], preferred_element_type=jnp.float32
        )
        out_ref[:, columns] = out.astype(jnp.bfloat16)


def own_hidden_kernel(rows_ref, gate_ref, up_ref, down_hbm, hidden_ref, bottom_ref, sem):
    depth = bottom_ref.shape[0]
    load = pltpu.make_async_copy(
        down_hbm.at[pl.ds(down_hbm.shape[0] - depth, depth)], bottom_ref, sem
    )
    load.start()
    shape = rows_ref.shape
    rows = rows_ref[...].reshape(shape[0] * shape[1], shape[2])
    fill_hidden(rows, gate_ref, up_ref, hidden_ref)
    load.wait()


def own_hidden(rows, gate, up, down, top):
    count = rows.shape[0] * rows.shape[1]
    return pl.pallas_call(
        own_hidden_kernel,
        out_shape=[
            jax.ShapeDtypeStruct((count, gate.shape[1]), jnp.bfloat16),
            pltpu.VMEM((down.shape[0] - top.shape[0], down.shape[1]), down.dtype),
        ],
        in_specs=[VMEM_SPEC] * 3 + [HBM_SPEC],
        out_specs=[VMEM_SPEC] * 2,
        scratch_shapes=[pltpu.SemaphoreType.DMA],
        compiler_params=pltpu.CompilerParams(vmem_limit_bytes=8 << 20),
        cost_estimate=pl.CostEstimate(
            flops=4 * count * gate.size, bytes_accessed=5 * gate.size, transcendentals=0
        ),
    )(place(rows), place(gate), place(up), stay(down))


def other_partial_kernel(rows_ref, gate_ref, up_ref, top_ref, bottom_ref, send_ref, hidden_ref):
    shape = rows_ref.shape
    rows = rows_ref[...].reshape(shape[0] * shape[1], shape[2])
    fill_hidden(rows, gate_ref, up_ref, hidden_ref)
    fill_partial(hidden_ref[...], top_ref, bottom_ref, send_ref)


def other_partial(rows, gate, up, top, bottom):
    count, feature = rows.shape[0] * rows.shape[1], rows.shape[2]
    return pl.pallas_call(
        other_partial_kernel,
        out_shape=jax.ShapeDtypeStruct((count, feature), jnp.bfloat16),
        in_specs=[VMEM_SPEC] * 5,
        out_specs=VMEM_SPEC,
        scratch_shapes=[pltpu.VMEM((count, gate.shape[1]), jnp.bfloat16)],
        compiler_params=pltpu.CompilerParams(vmem_limit_bytes=8 << 20),
    )(place(rows), place(gate), place(up), place(top), place(bottom))


def own_partial_kernel(hidden_ref, top_ref, bottom_ref, keep_ref):
    fill_partial(hidden_ref[...], top_ref, bottom_ref, keep_ref)


def own_partial(hidden, top, bottom):
    rows, feature = hidden.shape[0], top.shape[1]
    return pl.pallas_call(
        own_partial_kernel,
        out_shape=jax.ShapeDtypeStruct((rows, feature), jnp.bfloat16),
        in_specs=[VMEM_SPEC] * 3,
        out_specs=VMEM_SPEC,
        compiler_params=pltpu.CompilerParams(vmem_limit_bytes=4 << 20),
        cost_estimate=pl.CostEstimate(
            flops=4 * rows * top.size, bytes_accessed=4 * top.size, transcendentals=0
        ),
    )(place(hidden), place(top), place(bottom))


def swap_sides(block):
    return lax.ppermute(block, "side", [(0, 1), (1, 0)])


def local(
    queries,
    latent_cache,
    new_latent,
    lengths,
    residual,
    norm_gain,
    value_up,
    output_proj,
    expert_ids,
    expert_weights,
    gate_proj,
    up_proj,
    down_proj,
):
    row_count = queries.shape[0]
    feature = residual.shape[1]
    ep_count = lax.axis_size("ep")
    side_count = lax.axis_size("side")
    assert side_count == 2 and ep_count % 2 == 0 and ep_count <= 256
    flat_out = output_proj.reshape(output_proj.shape[0] * output_proj.shape[1], feature)
    capacity = min(
        row_count, max(2, (row_count * expert_ids.shape[1] + ep_count - 1) // ep_count)
    )

    latent, value_up, left = attend(
        queries, latent_cache, new_latent, lengths, value_up, flat_out, ep_count * side_count
    )
    arrived = lax.all_to_all(latent, ("ep", "side"), split_axis=0, concat_axis=0, tiled=True)
    send, own_heads, right = project_heads(arrived, value_up, left, flat_out)
    from_other = swap_sides(send)
    keep = project_own(own_heads, left, right)
    members = ep_count // 2
    zones = [list(range(members)), list(range(members, ep_count))]
    contribution = sum_halves(keep, from_other, members, 1)
    shared = lax.all_to_all(
        contribution, "ep", split_axis=0, concat_axis=0, tiled=True, axis_index_groups=zones
    )
    part, part_copy = fold(shared, residual, expert_ids)
    other_part = lax.ppermute(
        part_copy, "ep", [(e, (e + members) % ep_count) for e in range(ep_count)]
    )
    gate, up, top = load_weights(part_copy, gate_proj[0], up_proj[0], down_proj[0])
    outbound, stream, coefficient = route(
        part, other_part, norm_gain, expert_ids, expert_weights, gate, ep_count, capacity
    )
    own_rows = lax.all_to_all(
        outbound, "ep", split_axis=0, concat_axis=0, tiled=True, axis_index_groups=zones
    )
    other_rows = swap_sides(own_rows)
    hidden, bottom = own_hidden(own_rows, gate, up, down_proj[0], top)
    send = other_partial(other_rows, gate, up, top, bottom)
    other = swap_sides(send)
    keep = own_partial(hidden, top, bottom)
    both = sum_halves(keep, other, ep_count, 2)
    returned = lax.all_to_all(both, "ep", split_axis=0, concat_axis=0, tiled=True)
    return mix(returned, coefficient, stream)


def solution(mesh):
    in_specs = (
        P(("groups", "ep", "side"), None, None),
        P(("groups", "ep", "side"), None, None),
        P(("groups", "ep", "side"), None),
        P(("groups", "ep", "side")),
        P(("groups", "ep", "side"), None),
        P(),
        P(("ep", "side"), None, None),
        P(("ep", "side"), None, None),
        P(("groups", "ep", "side"), None),
        P(("groups", "ep", "side"), None),
        P("ep", None, "side"),
        P("ep", None, "side"),
        P("ep", "side", None),
    )
    out_specs = P(("groups", "ep", "side"), None)
    return jax.shard_map(local, mesh=mesh, in_specs=in_specs, out_specs=out_specs, check_vma=False)
```
